32 devices in a mesh: subj: 4 (over y, x), slab: 8 (over z, core).
Axes of the slice: x: 2, y: 2, z: 4, core: 2. Of those that a mesh axis runs over, the one named last changes fastest.
Arguments:
- source_bricks: bfloat16 [4, 64, 48000], P('subj', 'slab'), may hold values from -6 to 6
- brick_ids: int32 [4, 256], P('subj', 'slab'), may hold values from 0 to 63, as said below
- brick_offsets: int32 [4, 3, 256], P('subj', None, 'slab'), may hold values from 0 to 4
- deformation: float32 [4, 3, 32, 64, 128], P('subj', None, 'slab'), may hold values from -0.3 to 0.3
Outputs:
- atlas_mean: float32 [6, 32, 64, 128], P(None, 'slab', 'subj')
The draws below stay inside these ranges and needn't reach their ends.
Inputs may be any that keep to these rules, and one draw needn't show every extreme that they name: `brick_ids`: brick ids of slab k are k * 8 to (k + 1) * 8 - 1. Among the 32 template pieces of one slab and one subject, at most 6 source bricks lie in any one slab, and in every such list some slab is named exactly 6 times.
All inputs are finite; a program needn't handle non-finite values.
Results may differ from the reference program's by a relative error of at most 0.00095.
Values may be sent and summed in bfloat16 or wider, within the bound.
A program may use at most 128 MiB of HBM per device.

```python
import jax
import jax.numpy as jnp
from jax import lax

COMP = 6
BRICK = 16
PAD = 2
ZQ = 4
BX = 8
BY = 4
NEWTON = 2
NB_ROW = 32
SLAB_Z = 4
SB_DEV = 8
NBT = 64
PIECES = 256
CAP = 6
SUBJECTS = 4
NZ = 32
NY = 64
NX = 128
N_SLAB = 8


def draw_brick_ids(key, part):
    slab_count = PIECES // NB_ROW
    blocks = SUBJECTS * slab_count
    key_heavy, key_rest, key_order, key_local = jax.random.split(key, 4)
    heavy_owner = jax.random.randint(key_heavy, (blocks,), 0, slab_count)
    pool_size = (slab_count - 1) * CAP
    shuffled = jax.vmap(lambda sub_key: jax.random.permutation(sub_key, pool_size))(jax.random.split(key_rest, blocks))
    others = shuffled[:, :NB_ROW - CAP] // CAP
    others = others + (others >= heavy_owner[:, None]).astype(jnp.int32)
    owners = jnp.concatenate([jnp.broadcast_to(heavy_owner[:, None], (blocks, CAP)), others.astype(jnp.int32)], axis=1)
    ordering = jax.vmap(lambda sub_key: jax.random.permutation(sub_key, NB_ROW))(jax.random.split(key_order, blocks))
    owners = jnp.take_along_axis(owners, ordering, axis=1)
    local_index = jax.random.randint(key_local, (blocks, NB_ROW), 0, SB_DEV)
    return (owners * SB_DEV + local_index).reshape(SUBJECTS, PIECES).astype(jnp.int32)


def place_ends(drawn, stream_key, smallest, high):
    index_at = [jax.random.randint(jax.random.fold_in(stream_key, axis), (), 0, length) for axis, length in enumerate(drawn.shape)]
    longest = drawn.shape.index(max(drawn.shape))
    neighbour = index_at[:longest] + [(index_at[longest] + 1) % drawn.shape[longest]] + index_at[longest + 1:]
    return drawn.at[tuple(index_at)].set(smallest).at[tuple(neighbour)].set(high)


def block_scale(rng, dims, cuts, least, largest):
    level, own = 1.0, jax.random.fold_in(rng, 6)
    for position, parts in cuts:
        steps = jnp.exp(jax.random.uniform(jax.random.fold_in(own, position), (parts,), jnp.float32, least / len(cuts), largest / len(cuts)))
        level = level * jnp.repeat(steps, dims[position] // parts).reshape([-1 if axis == position else 1 for axis in range(len(dims))])
    return level


def centred(own_key, extent, spread, most, cuts=(), held_as=jnp.bfloat16):
    array = jax.random.normal(own_key, extent, jnp.float32) * spread
    if len(cuts) > 0:
        array = block_scale(own_key, extent, cuts, -0.22, 0.18) * array
    return jnp.clip(array, min=-most, max=most).astype(held_as)


def setup_inputs(seed: int = 0) -> dict:
    key_list = jax.random.split(jax.random.key(seed), 5)
    return {
        "source_bricks": centred(key_list[0], (SUBJECTS, NBT, COMP * (BRICK + 2 * PAD) ** 3), 1.0, 6.0, ((0, 4), (1, 8))),
        "brick_ids": draw_brick_ids(jax.random.fold_in(key_list[4], 71), 0),
        "brick_offsets": place_ends(jax.random.randint(key_list[2], (SUBJECTS, 3, PIECES), 0, 2 * PAD + 1), jax.random.fold_in(key_list[2], 1), 0, 2 * PAD).astype(jnp.int32),
        "deformation": centred(key_list[3], (SUBJECTS, 3, NZ, NY, NX), 0.1, 0.3, ((0, 4), (2, 8)), jnp.float32),
    }


def crop_window(flat_brick, start_z, start_y, start_x):
    edge_full = BRICK + 2 * PAD
    brick_cube = flat_brick.reshape(COMP, edge_full, edge_full, edge_full)
    anchor = jnp.zeros((), jnp.int32)
    window = lax.dynamic_slice(brick_cube, (anchor, start_z.astype(jnp.int32), start_y.astype(jnp.int32), start_x.astype(jnp.int32)), (COMP, SLAB_Z, BRICK, BRICK))
    return window.reshape(COMP * SLAB_Z * BRICK * BRICK)


def jacobian(rimmed):
    along_z = (rimmed[:, 2:, 1:-1, 1:-1] - rimmed[:, :-2, 1:-1, 1:-1]) * 0.5
    along_y = (rimmed[:, 1:-1, 2:, 1:-1] - rimmed[:, 1:-1, :-2, 1:-1]) * 0.5
    along_x = (rimmed[:, 1:-1, 1:-1, 2:] - rimmed[:, 1:-1, 1:-1, :-2]) * 0.5
    gradients = (along_z, along_y, along_x)
    return [[gradients[col_at][row_at] + (1.0 if row_at == col_at else 0.0) for col_at in range(3)] for row_at in range(3)]


def polar_factor(matrix):
    for newton_step in range(NEWTON):
        cofactor = [[matrix[(row_at + 1) % 3][(col_at + 1) % 3] * matrix[(row_at + 2) % 3][(col_at + 2) % 3]
                     - matrix[(row_at + 1) % 3][(col_at + 2) % 3] * matrix[(row_at + 2) % 3][(col_at + 1) % 3]
                     for col_at in range(3)] for row_at in range(3)]
        determinant = matrix[0][0] * cofactor[0][0] + matrix[0][1] * cofactor[0][1] + matrix[0][2] * cofactor[0][2]
        scaling = 1.0 / determinant
        matrix = [[0.5 * (matrix[row_at][col_at] + cofactor[row_at][col_at] * scaling) for col_at in range(3)] for row_at in range(3)]
    return matrix


def reorient(components, rotation):
    tensor_rows = [[components[0], components[3], components[4]],
                   [components[3], components[1], components[5]],
                   [components[4], components[5], components[2]]]
    left_side = [[rotation[row_at][0] * tensor_rows[0][col_at] + rotation[row_at][1] * tensor_rows[1][col_at]
                  + rotation[row_at][2] * tensor_rows[2][col_at] for col_at in range(3)] for row_at in range(3)]
    pair_list = ((0, 0), (1, 1), (2, 2), (0, 1), (0, 2), (1, 2))
    return [left_side[row_at][0] * rotation[col_at][0] + left_side[row_at][1] * rotation[col_at][1]
            + left_side[row_at][2] * rotation[col_at][2] for row_at, col_at in pair_list]


def reference(source_bricks, brick_ids, brick_offsets, deformation):
    total = jnp.zeros((COMP, NZ, NY, NX), jnp.float32)
    piece_index = jnp.arange(PIECES, dtype=jnp.int32)
    quarter_start = ((piece_index // NB_ROW) % ZQ) * SLAB_Z
    for subject in range(SUBJECTS):
        subject_bricks = source_bricks[subject]
        starts = brick_offsets[subject]

        def cut_piece(brick_id, start_z, start_y, start_x):
            return crop_window(subject_bricks[brick_id], start_z, start_y, start_x)

        windows = jax.vmap(cut_piece)(brick_ids[subject], quarter_start + starts[0], starts[1], starts[2])
        voxel_field = windows.reshape(N_SLAB, BY, BX, COMP, SLAB_Z, BRICK, BRICK)
        voxel_field = voxel_field.transpose(3, 0, 4, 1, 5, 2, 6).reshape(COMP, NZ, NY, NX)
        rimmed = jnp.pad(deformation[subject], ((0, 0), (1, 1), (1, 1), (1, 1)))
        rotation = polar_factor(jacobian(rimmed))
        tensor = voxel_field.astype(jnp.float32)
        rotated = reorient([tensor[channel] for channel in range(COMP)], rotation)
        total = total + jnp.stack(rotated)
    return total / SUBJECTS
```

```python
import functools

import jax
import jax.numpy as jnp
from jax import lax
from jax.experimental import pallas as pl
from jax.experimental.pallas import tpu as pltpu
from jax.sharding import PartitionSpec as P

COMP = 6
BRICK = 16
PAD = 2
EDGE = BRICK + 2 * PAD
ZQ = 4
NEWTON = 2
SLAB_Z = 4
LANES = 128
ROWS = COMP * SLAB_Z
BRICK_ROWS = COMP * EDGE
SPAN = 384
FLAT = BRICK * BRICK


def relayout_bricks(x_ref, rows_ref):
    held = x_ref.shape[0]
    lane = lax.broadcasted_iota(jnp.int32, (held, LANES), 1)
    group_lanes = 8 * EDGE * EDGE
    for group in range(BRICK_ROWS // 8):
        for m in range(8):
            cz = group * 8 + m
            c, z = cz // EDGE, cz % EDGE
            first = group * group_lanes + 3 * m * LANES
            shift = 16 * m
            tiles = []
            for j in range(4):
                tile = x_ref[:, first + j * LANES:first + (j + 1) * LANES].astype(jnp.float32)
                tiles.append(pltpu.roll(tile, LANES - shift, 1) if shift else tile)
            for j in range(4):
                value = tiles[j]
                if shift and j < 3:
                    value = jnp.where(lane < LANES - shift, tiles[j], tiles[j + 1])
                rows_ref[j, pl.ds(z * COMP + c, held, stride=BRICK_ROWS), :] = value


def selection():
    source = lax.broadcasted_iota(jnp.int32, (SPAN, FLAT), 0)
    target = lax.broadcasted_iota(jnp.int32, (SPAN, FLAT), 1)
    return (source == target // BRICK * EDGE + target % BRICK).astype(jnp.float32).astype(jnp.bfloat16)


def shifted_window(rows_ref, code):
    start, shift = code // LANES, code % LANES
    lane = lax.broadcasted_iota(jnp.int32, (ROWS, LANES), 1)
    rolled = [
        pltpu.roll(rows_ref[j, pl.ds(start, ROWS), :], (LANES - shift) % LANES, 1) for j in range(4)
    ]
    return [jnp.where(lane < LANES - shift, rolled[j], rolled[j + 1]) for j in range(3)]


def crop_kernel(code_ref, x_ref, out_ref, rows_ref, shifted_ref):
    relayout_bricks(x_ref, rows_ref)
    readers, chunk, _ = out_ref.shape
    capacity = chunk // ROWS
    select = selection()

    def step(reader, carry):
        for slot in range(capacity):
            window = shifted_window(rows_ref, code_ref[reader * capacity + slot])
            for j in range(3):
                shifted_ref[slot * ROWS:(slot + 1) * ROWS, j * LANES:(j + 1) * LANES] = window[j]
        out_ref[reader] = jnp.dot(
            shifted_ref[...].astype(jnp.bfloat16), select, preferred_element_type=jnp.float32
        ).astype(jnp.bfloat16)
        return carry

    lax.fori_loop(0, readers, step, 0)


def swap_groups(value):
    sub = lax.broadcasted_iota(jnp.int32, value.shape, 1)
    group = lax.broadcasted_iota(jnp.int32, value.shape, 2) // BRICK
    for bit in (1, 2, 4):
        from_below = pltpu.roll(pltpu.roll(value, 8 - bit, 1), BRICK * bit, 2)
        if bit == 4:
            from_above = from_below
        else:
            from_above = pltpu.roll(pltpu.roll(value, bit, 1), LANES - BRICK * bit, 2)
        low = (sub & bit) == 0
        same = (sub & bit) == (group & bit)
        value = jnp.where(same, value, jnp.where(low, from_below, from_above))
    return value


def place_row(slot_ref, wide_ref, turned_ref, row):
    across = LANES // BRICK
    for j in range(across):
        base = pl.multiple_of(slot_ref[row * across + j] * ROWS, 8)
        for h in range(2):
            for part in range(ROWS // 8):
                turned_ref[h, pl.ds(part * 64 + j, 8, stride=8), :] = wide_ref[
                    h, pl.ds(base + part * 8, 8), :
                ]
    return [swap_groups(turned_ref[h].reshape(ROWS, 8, LANES)) for h in range(2)]


def place_kernel(slot_ref, in_ref, out_ref, wide_ref, turned_ref):
    readers, chunk, _ = in_ref.shape

    def widen(reader, carry):
        base = pl.multiple_of(reader * chunk, 8)
        for h in range(2):
            wide_ref[h, pl.ds(base, chunk), :] = in_ref[
                reader, :, h * LANES:(h + 1) * LANES
            ].astype(jnp.float32)
        return carry

    lax.fori_loop(0, readers, widen, 0)

    def step(row, carry):
        halves = place_row(slot_ref, wide_ref, turned_ref, row)
        out_ref[row] = jnp.concatenate(halves, axis=1).astype(jnp.bfloat16)
        return carry

    lax.fori_loop(0, out_ref.shape[0], step, 0)


def polar_factor(matrix):
    for newton_step in range(NEWTON):
        cofactor = [
            [
                matrix[(a + 1) % 3][(b + 1) % 3] * matrix[(a + 2) % 3][(b + 2) % 3]
                - matrix[(a + 1) % 3][(b + 2) % 3] * matrix[(a + 2) % 3][(b + 1) % 3]
                for b in range(3)
            ]
            for a in range(3)
        ]
        determinant = (
            matrix[0][0] * cofactor[0][0]
            + matrix[0][1] * cofactor[0][1]
            + matrix[0][2] * cofactor[0][2]
        )
        scaling = 0.5 / determinant
        matrix = [
            [0.5 * matrix[a][b] + cofactor[a][b] * scaling for b in range(3)] for a in range(3)
        ]
    return matrix


def reorient(components, rotation):
    tensor_rows = [
        [components[0], components[3], components[4]],
        [components[3], components[1], components[5]],
        [components[4], components[5], components[2]],
    ]
    left_side = [
        [
            rotation[a][0] * tensor_rows[0][b]
            + rotation[a][1] * tensor_rows[1][b]
            + rotation[a][2] * tensor_rows[2][b]
            for b in range(3)
        ]
        for a in range(3)
    ]
    pair_list = ((0, 0), (1, 1), (2, 2), (0, 1), (0, 2), (1, 2))
    return [
        left_side[a][0] * rotation[b][0]
        + left_side[a][1] * rotation[b][1]
        + left_side[a][2] * rotation[b][2]
        for a, b in pair_list
    ]


def rotation_at(load):
    lane = lax.broadcasted_iota(jnp.int32, (BRICK, LANES), 1)
    matrix = []
    for a in range(3):
        here = load(a, 1)
        centre = here[1:BRICK + 1]
        along_z = (load(a, 2)[1:BRICK + 1] - load(a, 0)[1:BRICK + 1]) * 0.5
        along_y = (here[2:BRICK + 2] - here[0:BRICK]) * 0.5
        later = jnp.where(lane == LANES - 1, 0.0, pltpu.roll(centre, LANES - 1, 1))
        earlier = jnp.where(lane == 0, 0.0, pltpu.roll(centre, 1, 1))
        gradients = [along_z, along_y, (later - earlier) * 0.5]
        gradients[a] = gradients[a] + 1.0
        matrix.append(gradients)
    return polar_factor(matrix)


def mean_kernel(field_ref, u_ref, out_ref):
    subjects = field_ref.shape[0]

    def step(z, carry):
        total = None
        for s in range(subjects):
            rotation = rotation_at(lambda a, dz: u_ref[s, a, z + dz].astype(jnp.float32))
            tensor = [field_ref[s, z * COMP + c].astype(jnp.float32) for c in range(COMP)]
            rotated = reorient(tensor, rotation)
            total = rotated if total is None else [p + q for p, q in zip(total, rotated)]
        for c in range(COMP):
            out_ref[c, z] = total[c] * (1.0 / subjects)
        return carry

    lax.fori_loop(0, SLAB_Z, step, 0)


VMEM_SPEC = pl.BlockSpec(memory_space=pltpu.VMEM)
SMEM_SPEC = pl.BlockSpec(memory_space=pltpu.SMEM)
PARAMS = pltpu.CompilerParams(vmem_limit_bytes=40 << 20)


def slot_tables(brick_ids, brick_offsets, held, slab_count, capacity):
    wanted = brick_ids[0]
    pieces = wanted.shape[0]
    owner, local = wanted // held, wanted % held
    positions = jnp.arange(pieces, dtype=jnp.int32)
    earlier = (owner[:, None] == owner[None, :]) & (positions[None, :] < positions[:, None])
    slot_of = owner * capacity + jnp.sum(earlier.astype(jnp.int32), axis=1)
    start_z = brick_offsets[0, 0] + lax.axis_index("slab") % ZQ * SLAB_Z
    shift = brick_offsets[0, 1] * EDGE + brick_offsets[0, 2]
    code = (local * BRICK_ROWS + start_z * COMP) * LANES + shift
    hits = slot_of[:, None] == jnp.arange(slab_count * capacity, dtype=jnp.int32)[None, :]
    return slot_of, jnp.sum(jnp.where(hits, code[:, None], 0), axis=0)


def row_windows(deformation, subjects):
    u = deformation[0].astype(jnp.bfloat16)
    count = lax.axis_size("slab")
    before = lax.ppermute(u[:, -1:], "slab", [(i, i + 1) for i in range(count - 1)])
    after = lax.ppermute(u[:, :1], "slab", [(i + 1, i) for i in range(count - 1)])
    u = jnp.concatenate([before, u, after], axis=1)
    u = jnp.pad(u, ((0, 0), (0, 0), (1, 1), (0, 0)))
    blocks = jnp.stack([u[:, :, r * BRICK:r * BRICK + BRICK + 2] for r in range(subjects)])
    return lax.all_to_all(blocks, "subj", split_axis=0, concat_axis=0, tiled=True)


def shards(source_bricks, brick_ids, brick_offsets, deformation):
    slab_count, subjects = lax.axis_size("slab"), lax.axis_size("subj")
    pieces = brick_ids.shape[1]
    held = source_bricks.shape[1]
    capacity = max(2, 3 * pieces // (2 * slab_count))
    chunk = capacity * ROWS
    slot_of, code = slot_tables(brick_ids, brick_offsets, held, slab_count, capacity)
    asked = lax.all_to_all(
        code.reshape(slab_count, capacity), "slab", split_axis=0, concat_axis=0, tiled=True
    ).reshape(-1)
    rows = row_windows(deformation, subjects)
    cropped = pl.pallas_call(
        crop_kernel,
        out_shape=jax.ShapeDtypeStruct((slab_count, chunk, FLAT), jnp.bfloat16),
        in_specs=[SMEM_SPEC, VMEM_SPEC],
        out_specs=VMEM_SPEC,
        scratch_shapes=[
            pltpu.VMEM((4, held * BRICK_ROWS, LANES), jnp.float32),
            pltpu.VMEM((chunk, SPAN), jnp.float32),
        ],
        compiler_params=PARAMS,
    )(asked, source_bricks[0])
    arrived = lax.all_to_all(cropped, "slab", split_axis=0, concat_axis=0, tiled=True)
    rows_y = pieces // (deformation.shape[4] // BRICK)
    placed = pl.pallas_call(
        place_kernel,
        out_shape=jax.ShapeDtypeStruct((rows_y, ROWS, BRICK, LANES), jnp.bfloat16),
        in_specs=[SMEM_SPEC, VMEM_SPEC],
        out_specs=VMEM_SPEC,
        scratch_shapes=[
            pltpu.VMEM((2, slab_count * chunk, LANES), jnp.float32),
            pltpu.VMEM((2, ROWS * 8, LANES), jnp.float32),
        ],
        compiler_params=PARAMS,
    )(slot_of, arrived)
    fields = lax.all_to_all(placed, "subj", split_axis=0, concat_axis=0, tiled=True)
    return pl.pallas_call(
        mean_kernel,
        out_shape=jax.ShapeDtypeStruct((COMP, SLAB_Z, BRICK, LANES), jnp.float32),
        in_specs=[VMEM_SPEC, VMEM_SPEC],
        out_specs=VMEM_SPEC,
        compiler_params=PARAMS,
    )(fields, rows)


def solution(mesh):
    in_specs = (
        P("subj", "slab", None),
        P("subj", "slab"),
        P("subj", None, "slab"),
        P("subj", None, "slab", None, None),
    )
    out_specs = P(None, "slab", "subj", None)
    return jax.shard_map(shards, mesh=mesh, in_specs=in_specs, out_specs=out_specs, check_vma=False)
```

```python
import jax
import jax.numpy as jnp
from jax import lax
from jax.experimental import pallas as pl
from jax.experimental.pallas import tpu as pltpu
from jax.sharding import PartitionSpec as P

COMP = 6
BRICK = 16
PAD = 2
EDGE = BRICK + 2 * PAD
ZQ = 4
NEWTON = 2
SLAB_Z = 4
LANES = 128
ROWS = COMP * SLAB_Z
BRICK_ROWS = COMP * EDGE
SPAN = 384
FLAT = BRICK * BRICK


def relayout_bricks(x_ref, rows_ref):
    held = x_ref.shape[0]
    lane = lax.broadcasted_iota(jnp.int32, (held, LANES), 1)
    group_lanes = 8 * EDGE * EDGE

    def step(group, carry):
        for m in range(8):
            cz = group * 8 + m
            row = cz % EDGE * COMP + cz // EDGE
            shift = 16 * m
            tiles = []
            for j in range(4):
                first = pl.multiple_of(group * group_lanes + (3 * m + j) * LANES, LANES)
                tile = x_ref[:, pl.ds(first, LANES)].astype(jnp.float32)
                tiles.append(pltpu.roll(tile, LANES - shift, 1) if shift else tile)
            for j in range(4):
                value = tiles[j]
                if shift and j < 3:
                    value = jnp.where(lane < LANES - shift, tiles[j], tiles[j + 1])
                rows_ref[j, pl.ds(row, held, stride=BRICK_ROWS), :] = value
        return carry

    lax.fori_loop(0, BRICK_ROWS // 8, step, 0)


def selection():
    source = lax.broadcasted_iota(jnp.int32, (SPAN, FLAT), 0)
    target = lax.broadcasted_iota(jnp.int32, (SPAN, FLAT), 1)
    return (source == target // BRICK * EDGE + target % BRICK).astype(jnp.float32).astype(jnp.bfloat16)


def crop_rows(codes, capacity, rows, select):
    depth = rows.shape[0]
    row = lax.broadcasted_iota(jnp.int32, (ROWS, depth), 0)
    column = lax.broadcasted_iota(jnp.int32, (ROWS, depth), 1)
    hits, shifts = [], []
    for slot in range(capacity):
        code = codes[:, slot:slot + 1]
        start = lax.shift_right_logical(code, jnp.full(code.shape, 7, jnp.int32))
        hits.append((column - row == jnp.broadcast_to(start, (ROWS, depth))).astype(jnp.float32))
        shifts.append(jnp.broadcast_to(code & (LANES - 1), (ROWS, LANES)))
    hit = jnp.concatenate(hits, axis=0).astype(jnp.bfloat16)
    shift = jnp.concatenate(shifts, axis=0)
    found = jnp.dot(hit, rows, preferred_element_type=jnp.float32)
    tiles = [found[:, j * LANES:(j + 1) * LANES] for j in range(4)]
    for bit in (1, 2, 4, 8, 16, 32, 64):
        taken = (shift & bit) != 0
        tiles = [jnp.where(taken, pltpu.roll(tile, LANES - bit, 1), tile) for tile in tiles]
    inside = lax.broadcasted_iota(jnp.int32, shift.shape, 1) + shift < LANES
    shifted = [jnp.where(inside, tiles[j], tiles[j + 1]).astype(jnp.bfloat16) for j in range(3)]
    return jnp.dot(jnp.concatenate(shifted, axis=1), select, preferred_element_type=jnp.float32)


def swap_groups(value):
    sub = lax.broadcasted_iota(jnp.int32, value.shape, 1)
    group = lax.broadcasted_iota(jnp.int32, value.shape, 2) // BRICK
    for bit in (1, 2, 4):
        from_below = pltpu.roll(pltpu.roll(value, 8 - bit, 1), BRICK * bit, 2)
        if bit == 4:
            from_above = from_below
        else:
            from_above = pltpu.roll(pltpu.roll(value, bit, 1), LANES - BRICK * bit, 2)
        low = (sub & bit) == 0
        same = (sub & bit) == (group & bit)
        value = jnp.where(same, value, jnp.where(low, from_below, from_above))
    return value


def place_row(slot_ref, arrived, row):
    across = LANES // BRICK
    depth = arrived.shape[0] * arrived.shape[1]
    sub = lax.broadcasted_iota(jnp.int32, (8, depth), 0)
    base = jnp.zeros((8, depth), jnp.int32)
    for j in range(across):
        base = jnp.where(sub == j, slot_ref[row * across + j] * ROWS, base)
    offset = lax.broadcasted_iota(jnp.int32, (8, depth), 1) - base
    hit = jnp.concatenate([(offset == n).astype(jnp.float32) for n in range(ROWS)], axis=0)
    pieces = jnp.dot(
        hit.astype(jnp.bfloat16), arrived[...].reshape(depth, FLAT), preferred_element_type=jnp.float32
    )
    return [
        swap_groups(pieces[:, h * LANES:(h + 1) * LANES].reshape(ROWS, 8, LANES)) for h in range(2)
    ]


def polar_factor(matrix):
    for newton_step in range(NEWTON):
        cofactor = [
            [
                matrix[(a + 1) % 3][(b + 1) % 3] * matrix[(a + 2) % 3][(b + 2) % 3]
                - matrix[(a + 1) % 3][(b + 2) % 3] * matrix[(a + 2) % 3][(b + 1) % 3]
                for b in range(3)
            ]
            for a in range(3)
        ]
        determinant = (
            matrix[0][0] * cofactor[0][0]
            + matrix[0][1] * cofactor[0][1]
            + matrix[0][2] * cofactor[0][2]
        )
        scaling = 0.5 / determinant
        matrix = [
            [0.5 * matrix[a][b] + cofactor[a][b] * scaling for b in range(3)] for a in range(3)
        ]
    return matrix


def reorient(components, rotation):
    tensor_rows = [
        [components[0], components[3], components[4]],
        [components[3], components[1], components[5]],
        [components[4], components[5], components[2]],
    ]
    left_side = [
        [
            rotation[a][0] * tensor_rows[0][b]
            + rotation[a][1] * tensor_rows[1][b]
            + rotation[a][2] * tensor_rows[2][b]
            for b in range(3)
        ]
        for a in range(3)
    ]
    pair_list = ((0, 0), (1, 1), (2, 2), (0, 1), (0, 2), (1, 2))
    return [
        left_side[a][0] * rotation[b][0]
        + left_side[a][1] * rotation[b][1]
        + left_side[a][2] * rotation[b][2]
        for a, b in pair_list
    ]


def rotation_at(load):
    lane = lax.broadcasted_iota(jnp.int32, (BRICK, LANES), 1)
    matrix = []
    for a in range(3):
        here = load(a, 1)
        centre = here[1:BRICK + 1]
        along_z = (load(a, 2)[1:BRICK + 1] - load(a, 0)[1:BRICK + 1]) * 0.5
        along_y = (here[2:BRICK + 2] - here[0:BRICK]) * 0.5
        later = jnp.where(lane == LANES - 1, 0.0, pltpu.roll(centre, LANES - 1, 1))
        earlier = jnp.where(lane == 0, 0.0, pltpu.roll(centre, 1, 1))
        gradients = [along_z, along_y, (later - earlier) * 0.5]
        gradients[a] = gradients[a] + 1.0
        matrix.append(gradients)
    return polar_factor(matrix)


def warp_kernel(
    code_ref, slot_ref, brick_ref, u_ref, out_ref,
    asked, rows_ref, rows_half, crops, arrived,
    u_pad, u_rows, u_all, rotations, placed, fields,
    ask_send, ask_recv, crop_send, crop_recv, u_send, u_recv, up_send, up_recv,
    down_send, down_recv, field_send, field_recv,
):
    count, subjects = arrived.shape[0], fields.shape[0]
    chunk = arrived.shape[1]
    capacity = chunk // ROWS
    me_s, me_k = lax.axis_index("subj"), lax.axis_index("slab")
    barrier = pltpu.get_barrier_semaphore()
    has_before, has_after = me_k > 0, me_k < count - 1

    def peer_slab(t):
        turn = (t + 1) // 2
        return (me_k + count // 2 + turn * (1 - 2 * ((t + 1) % 2)) + count) % count

    def peer_subj(t):
        return (me_s + t) % subjects

    def greet(s, k):
        pl.semaphore_signal(barrier, inc=1, device_id=(s, k), device_id_type=MESH)

    def greet_slab(t, carry):
        greet(me_s, peer_slab(t))
        return carry

    lax.fori_loop(0, count - 1, greet_slab, 0)
    for t in range(1, subjects):
        greet(peer_subj(t), me_k)

    @pl.when(has_before)
    def _():
        for t in range(1, subjects):
            greet(peer_subj(t), me_k - 1)

    @pl.when(has_after)
    def _():
        for t in range(1, subjects):
            greet(peer_subj(t), me_k + 1)

    def remote(source, target, send, recv, s, k):
        return pltpu.make_async_remote_copy(
            src_ref=source, dst_ref=target, send_sem=send, recv_sem=recv,
            device_id=(s, k), device_id_type=MESH,
        )

    edge = jnp.zeros((8, LANES), jnp.float32)
    height = u_ref.shape[2]

    def pad_rows(at, carry):
        a, z = at // SLAB_Z, at % SLAB_Z
        u_pad[0:8, :] = edge
        u_pad[8:8 + height, :] = u_ref[a, z]
        u_pad[8 + height:16 + height, :] = edge
        for r in range(subjects):
            first = 7 + r * BRICK
            u_rows[r, a, z] = u_pad[first:first + BRICK + 2, :].astype(jnp.bfloat16)
        return carry

    lax.fori_loop(0, 3 * SLAB_Z, pad_rows, 0)

    neighbours = (me_k + count - 1) // count + (2 * count - 2 - me_k) // count
    pl.semaphore_wait(barrier, count - 1 + (subjects - 1) * (1 + neighbours))

    def ask(k):
        return remote(code_ref.at[k], asked.at[me_k], ask_send.at[k], ask_recv.at[me_k], me_s, k)

    def ask_from(k):
        return remote(code_ref.at[k], asked.at[k], ask_send.at[k], ask_recv.at[k], me_s, k)

    def start_ask(t, carry):
        ask(peer_slab(t)).start()
        return carry

    lax.fori_loop(0, count - 1, start_ask, 0)
    asked[me_k] = code_ref[me_k]

    def u_block(r):
        return remote(
            u_rows.at[r], u_all.at[me_s, :, pl.ds(1, SLAB_Z)], u_send.at[r], u_recv.at[me_s], r, me_k
        )

    def u_block_from(s):
        return remote(
            u_rows.at[s], u_all.at[s, :, pl.ds(1, SLAB_Z)], u_send.at[s], u_recv.at[s], s, me_k
        )

    def u_before(r, s):
        return remote(
            u_rows.at[r, :, pl.ds(0, 1)], u_all.at[s, :, pl.ds(SLAB_Z + 1, 1)],
            up_send.at[r], up_recv.at[s], r, me_k - 1,
        )

    def u_after(r, s):
        return remote(
            u_rows.at[r, :, pl.ds(SLAB_Z - 1, 1)], u_all.at[s, :, pl.ds(0, 1)],
            down_send.at[r], down_recv.at[s], r, me_k + 1,
        )

    for t in range(1, subjects):
        u_block(peer_subj(t)).start()

    @pl.when(has_before)
    def _():
        for t in range(subjects):
            u_before(peer_subj(t), me_s).start()

    @pl.when(has_after)
    def _():
        for t in range(subjects):
            u_after(peer_subj(t), me_s).start()

    def keep_u(at, carry):
        a, z = at // SLAB_Z, at % SLAB_Z
        u_all[me_s, a, z + 1] = u_rows[me_s, a, z]
        return carry

    lax.fori_loop(0, 3 * SLAB_Z, keep_u, 0)
    rim = jnp.zeros((BRICK + 2, LANES), jnp.bfloat16)

    @pl.when(me_k == 0)
    def _():
        for s in range(subjects):
            for a in range(3):
                u_all[s, a, 0] = rim

    @pl.when(me_k == count - 1)
    def _():
        for s in range(subjects):
            for a in range(3):
                u_all[s, a, SLAB_Z + 1] = rim

    relayout_bricks(brick_ref, rows_ref)
    for j in range(4):
        rows_half[:, j * LANES:(j + 1) * LANES] = rows_ref[j].astype(jnp.bfloat16)
    select = selection()

    def wait_ask(t, carry):
        ask_from(peer_slab(t)).wait_recv()
        return carry

    lax.fori_loop(0, count - 1, wait_ask, 0)
    def crop(k):
        return crop_rows(asked[k], capacity, rows_half[...], select).astype(jnp.bfloat16)

    def give(k):
        return remote(crops.at[k], arrived.at[me_k], crop_send.at[k], crop_recv.at[me_k], me_s, k)

    def take(k):
        return remote(crops.at[k], arrived.at[k], crop_send.at[k], crop_recv.at[k], me_s, k)

    def crop_and_give(t, carry):
        reader = peer_slab(t)
        crops[reader] = crop(reader)
        give(reader).start()
        return carry

    lax.fori_loop(0, count - 1, crop_and_give, 0)

    arrived[me_k] = crop(me_k)

    for t in range(1, subjects):
        u_block_from(peer_subj(t)).wait_recv()

    @pl.when(has_before)
    def _():
        for t in range(subjects):
            u_after(peer_subj(t), peer_subj(t)).wait_recv()

    @pl.when(has_after)
    def _():
        for t in range(subjects):
            u_before(peer_subj(t), peer_subj(t)).wait_recv()

    def rotate(at, carry):
        s, z = at // SLAB_Z, at % SLAB_Z
        rotation = rotation_at(lambda a, dz: u_all[s, a, z + dz].astype(jnp.float32))
        for a in range(3):
            for b in range(3):
                rotations[s, z, a * 3 + b] = rotation[a][b]
        return carry

    lax.fori_loop(0, subjects * SLAB_Z, rotate, 0)

    def collect(t, carry):
        take(peer_slab(t)).wait_recv()
        return carry

    lax.fori_loop(0, count - 1, collect, 0)

    def share(r):
        return remote(
            placed.at[r], fields.at[me_s], field_send.at[r], field_recv.at[me_s], r, me_k
        )

    def shared_from(s):
        return remote(placed.at[s], fields.at[s], field_send.at[s], field_recv.at[s], s, me_k)

    def place(row):
        halves = place_row(slot_ref, arrived, row)
        return jnp.concatenate(halves, axis=1).astype(jnp.bfloat16)

    def place_and_share(t, carry):
        r = peer_subj(t)
        placed[r] = place(r)
        share(r).start()
        return carry

    lax.fori_loop(1, subjects, place_and_share, 0)
    fields[me_s] = place(me_s)

    def add_subject(t, first):
        s = peer_subj(t)

        def step(z, carry):
            rotation = [[rotations[s, z, a * 3 + b] for b in range(3)] for a in range(3)]
            tensor = [
                fields[s, z * COMP + c].astype(jnp.float32) * (1.0 / subjects) for c in range(COMP)
            ]
            rotated = reorient(tensor, rotation)
            for c in range(COMP):
                out_ref[c, z] = rotated[c] if first else out_ref[c, z] + rotated[c]
            return carry

        lax.fori_loop(0, SLAB_Z, step, 0)

    add_subject(0, True)
    for t in range(1, subjects):
        shared_from(peer_subj(t)).wait_recv()
        add_subject(t, False)

    def finish(t, carry):
        k = peer_slab(t)
        ask(k).wait_send()
        give(k).wait_send()
        return carry

    lax.fori_loop(0, count - 1, finish, 0)
    for t in range(1, subjects):
        u_block(peer_subj(t)).wait_send()
        share(peer_subj(t)).wait_send()

    @pl.when(has_before)
    def _():
        for t in range(subjects):
            u_before(peer_subj(t), me_s).wait_send()

    @pl.when(has_after)
    def _():
        for t in range(subjects):
            u_after(peer_subj(t), me_s).wait_send()


MESH = pl.DeviceIdType.MESH
VMEM_SPEC = pl.BlockSpec(memory_space=pltpu.VMEM)
SMEM_SPEC = pl.BlockSpec(memory_space=pltpu.SMEM)


def slot_tables(brick_ids, brick_offsets, held, slab_count, capacity):
    wanted = brick_ids[0]
    pieces = wanted.shape[0]
    owner, local = wanted // held, wanted % held
    positions = jnp.arange(pieces, dtype=jnp.int32)
    earlier = (owner[:, None] == owner[None, :]) & (positions[None, :] < positions[:, None])
    slot_of = owner * capacity + jnp.sum(earlier.astype(jnp.int32), axis=1)
    start_z = brick_offsets[0, 0] + lax.axis_index("slab") % ZQ * SLAB_Z
    shift = brick_offsets[0, 1] * EDGE + brick_offsets[0, 2]
    code = (local * BRICK_ROWS + start_z * COMP) * LANES + shift
    hits = slot_of[:, None] == jnp.arange(slab_count * capacity, dtype=jnp.int32)[None, :]
    return slot_of, jnp.sum(jnp.where(hits, code[:, None], 0), axis=0)


def shards(source_bricks, brick_ids, brick_offsets, deformation):
    slab_count, subjects = lax.axis_size("slab"), lax.axis_size("subj")
    pieces = brick_ids.shape[1]
    held = source_bricks.shape[1]
    capacity = max(2, 3 * pieces // (2 * slab_count))
    chunk = capacity * ROWS
    slot_of, code = slot_tables(brick_ids, brick_offsets, held, slab_count, capacity)
    code = jnp.pad(code.reshape(slab_count, 1, capacity), ((0, 0), (0, 0), (0, LANES - capacity)))
    rim_rows = BRICK + 2
    bf16, f32, dma = jnp.bfloat16, jnp.float32, pltpu.SemaphoreType.DMA
    per_slab, per_subject = dma((slab_count,)), dma((subjects,))
    return pl.pallas_call(
        warp_kernel,
        out_shape=jax.ShapeDtypeStruct((COMP, SLAB_Z, BRICK, LANES), f32),
        in_specs=[VMEM_SPEC, SMEM_SPEC, VMEM_SPEC, VMEM_SPEC],
        out_specs=VMEM_SPEC,
        scratch_shapes=[
            pltpu.VMEM((slab_count, 1, LANES), jnp.int32),
            pltpu.VMEM((4, held * BRICK_ROWS, LANES), f32),
            pltpu.VMEM((held * BRICK_ROWS, 4 * LANES), bf16),
            pltpu.VMEM((slab_count, chunk, FLAT), bf16),
            pltpu.VMEM((slab_count, chunk, FLAT), bf16),
            pltpu.VMEM((deformation.shape[3] + 16, LANES), f32),
            pltpu.VMEM((subjects, 3, SLAB_Z, rim_rows, LANES), bf16),
            pltpu.VMEM((subjects, 3, SLAB_Z + 2, rim_rows, LANES), bf16),
            pltpu.VMEM((subjects, SLAB_Z, 9, BRICK, LANES), f32),
            pltpu.VMEM((subjects, ROWS, BRICK, LANES), bf16),
            pltpu.VMEM((subjects, ROWS, BRICK, LANES), bf16),
            per_slab, per_slab, per_slab, per_slab,
            per_subject, per_subject, per_subject, per_subject,
            per_subject, per_subject, per_subject, per_subject,
        ],
        compiler_params=pltpu.CompilerParams(
            vmem_limit_bytes=48 << 20, collective_id=0, has_side_effects=True
        ),
    )(code, slot_of, source_bricks[0], deformation[0])


def solution(mesh):
    in_specs = (
        P("subj", "slab", None),
        P("subj", "slab"),
        P("subj", None, "slab"),
        P("subj", None, "slab", None, None),
    )
    out_specs = P(None, "slab", "subj", None)
    return jax.shard_map(shards, mesh=mesh, in_specs=in_specs, out_specs=out_specs, check_vma=False)
```

```python
import jax
import jax.numpy as jnp
from jax import lax
from jax.experimental import pallas as pl
from jax.experimental.pallas import tpu as pltpu
from jax.sharding import PartitionSpec as P

COMP = 6
BRICK = 16
PAD = 2
EDGE = BRICK + 2 * PAD
ZQ = 4
NEWTON = 2
SLAB_Z = 4
LANES = 128
ROWS = COMP * SLAB_Z
BRICK_ROWS = COMP * EDGE
PARTS = COMP // 2
PART_ROWS = 2 * SLAB_Z
SPAN = 384
FLAT = BRICK * BRICK


def relayout_bricks(x_ref, rows_ref):
    held = x_ref.shape[0]
    lane = lax.broadcasted_iota(jnp.int32, (held, LANES), 1)
    group_lanes = 8 * EDGE * EDGE

    def step(group, carry):
        for m in range(8):
            cz = group * 8 + m
            row = cz % EDGE * COMP + cz // EDGE
            shift = 16 * m
            tiles = []
            for j in range(4):
                first = pl.multiple_of(group * group_lanes + (3 * m + j) * LANES, LANES)
                tile = x_ref[:, pl.ds(first, LANES)].astype(jnp.float32)
                tiles.append(pltpu.roll(tile, LANES - shift, 1) if shift else tile)
            for j in range(4):
                value = tiles[j]
                if shift and j < 3:
                    value = jnp.where(lane < LANES - shift, tiles[j], tiles[j + 1])
                rows_ref[j, pl.ds(row, held, stride=BRICK_ROWS), :] = value
        return carry

    lax.fori_loop(0, BRICK_ROWS // 8, step, 0)


def selection():
    source = lax.broadcasted_iota(jnp.int32, (SPAN, FLAT), 0)
    target = lax.broadcasted_iota(jnp.int32, (SPAN, FLAT), 1)
    return (source == target // BRICK * EDGE + target % BRICK).astype(jnp.float32).astype(jnp.bfloat16)


def crop_rows(codes, capacity, rows, select):
    depth = rows.shape[0]
    row = lax.broadcasted_iota(jnp.int32, (PART_ROWS, depth), 0)
    offset = lax.broadcasted_iota(jnp.int32, (PART_ROWS, depth), 1) - (row // 2 * COMP + row % 2)
    hits, shifts = [], []
    for slot in range(capacity):
        code = codes[:, slot:slot + 1]
        start = lax.shift_right_logical(code, jnp.full(code.shape, 7, jnp.int32))
        hits.append(offset - jnp.broadcast_to(start, (PART_ROWS, depth)))
        shifts.append(jnp.broadcast_to(code & (LANES - 1), (PART_ROWS, LANES)))
    hit = jnp.concatenate(
        [(hits[slot] == 2 * part).astype(jnp.float32) for part in range(PARTS) for slot in range(capacity)],
        axis=0,
    ).astype(jnp.bfloat16)
    shift = jnp.concatenate(shifts * PARTS, axis=0)
    found = jnp.dot(hit, rows, preferred_element_type=jnp.float32)
    tiles = [found[:, j * LANES:(j + 1) * LANES] for j in range(4)]
    for bit in (1, 2, 4, 8, 16, 32, 64):
        taken = (shift & bit) != 0
        tiles = [jnp.where(taken, pltpu.roll(tile, LANES - bit, 1), tile) for tile in tiles]
    inside = lax.broadcasted_iota(jnp.int32, shift.shape, 1) + shift < LANES
    shifted = [jnp.where(inside, tiles[j], tiles[j + 1]).astype(jnp.bfloat16) for j in range(3)]
    return jnp.dot(jnp.concatenate(shifted, axis=1), select, preferred_element_type=jnp.float32)


def swap_groups(value):
    sub = lax.broadcasted_iota(jnp.int32, value.shape, 1)
    group = lax.broadcasted_iota(jnp.int32, value.shape, 2) // BRICK
    for bit in (1, 2, 4):
        from_below = pltpu.roll(pltpu.roll(value, 8 - bit, 1), BRICK * bit, 2)
        if bit == 4:
            from_above = from_below
        else:
            from_above = pltpu.roll(pltpu.roll(value, bit, 1), LANES - BRICK * bit, 2)
        low = (sub & bit) == 0
        same = (sub & bit) == (group & bit)
        value = jnp.where(same, value, jnp.where(low, from_below, from_above))
    return value


def placing_hits(slot_ref, row, depth):
    across = LANES // BRICK
    sub = lax.broadcasted_iota(jnp.int32, (across, depth), 0)
    base = jnp.zeros((across, depth), jnp.int32)
    for j in range(across):
        base = jnp.where(sub == j, slot_ref[row * across + j] * PART_ROWS, base)
    offset = lax.broadcasted_iota(jnp.int32, (across, depth), 1) - base
    return jnp.concatenate(
        [(offset == n).astype(jnp.float32) for n in range(PART_ROWS)], axis=0
    ).astype(jnp.bfloat16)


def place_row(hit, windows):
    pieces = jnp.dot(hit, windows, preferred_element_type=jnp.float32)
    halves = [
        swap_groups(pieces[:, h * LANES:(h + 1) * LANES].reshape(PART_ROWS, 8, LANES))
        for h in range(2)
    ]
    return jnp.concatenate(halves, axis=1).astype(jnp.bfloat16)


def polar_factor(matrix):
    for newton_step in range(NEWTON):
        cofactor = [
            [
                matrix[(a + 1) % 3][(b + 1) % 3] * matrix[(a + 2) % 3][(b + 2) % 3]
                - matrix[(a + 1) % 3][(b + 2) % 3] * matrix[(a + 2) % 3][(b + 1) % 3]
                for b in range(3)
            ]
            for a in range(3)
        ]
        determinant = (
            matrix[0][0] * cofactor[0][0]
            + matrix[0][1] * cofactor[0][1]
            + matrix[0][2] * cofactor[0][2]
        )
        scaling = 0.5 / determinant
        matrix = [
            [0.5 * matrix[a][b] + cofactor[a][b] * scaling for b in range(3)] for a in range(3)
        ]
    return matrix


def reorient(components, rotation):
    tensor_rows = [
        [components[0], components[3], components[4]],
        [components[3], components[1], components[5]],
        [components[4], components[5], components[2]],
    ]
    left_side = [
        [
            rotation[a][0] * tensor_rows[0][b]
            + rotation[a][1] * tensor_rows[1][b]
            + rotation[a][2] * tensor_rows[2][b]
            for b in range(3)
        ]
        for a in range(3)
    ]
    pair_list = ((0, 0), (1, 1), (2, 2), (0, 1), (0, 2), (1, 2))
    return [
        left_side[a][0] * rotation[b][0]
        + left_side[a][1] * rotation[b][1]
        + left_side[a][2] * rotation[b][2]
        for a, b in pair_list
    ]


def rotation_at(centre, before, after):
    lane = lax.broadcasted_iota(jnp.int32, (BRICK, LANES), 1)
    matrix = []
    for a in range(3):
        here = centre[a][1:BRICK + 1]
        along_z = (after[a] - before[a]) * 0.5
        along_y = (centre[a][2:BRICK + 2] - centre[a][0:BRICK]) * 0.5
        later = jnp.where(lane == LANES - 1, 0.0, pltpu.roll(here, LANES - 1, 1))
        earlier = jnp.where(lane == 0, 0.0, pltpu.roll(here, 1, 1))
        gradients = [along_z, along_y, (later - earlier) * 0.5]
        gradients[a] = gradients[a] + 1.0
        matrix.append(gradients)
    return polar_factor(matrix)


def warp_kernel(
    code_ref, slot_ref, brick_hbm, u_hbm, out_ref,
    brick_ref, u_ref, asked, rows_ref, rows_half, crops, arrived, hits,
    u_pad, u_rows, u_edge, u_all, u_rim, rotations, placed, fields, load_sem,
    ask_send, ask_recv, crop_send, crop_recv, u_send, u_recv, up_send, up_recv,
    down_send, down_recv, field_send, field_recv,
):
    count, subjects = arrived.shape[1], fields.shape[0]
    capacity = arrived.shape[2] // PART_ROWS
    load_u = pltpu.make_async_copy(u_hbm.at[0], u_ref, load_sem.at[0])
    load_u.start()
    load_bricks = pltpu.make_async_copy(brick_hbm.at[0], brick_ref, load_sem.at[1])
    load_bricks.start()
    me_s, me_k = lax.axis_index("subj"), lax.axis_index("slab")
    barrier = pltpu.get_barrier_semaphore()
    has_before, has_after = me_k > 0, me_k < count - 1

    def peer_slab(t):
        turn = (t + 1) // 2
        return (me_k + count // 2 + turn * (1 - 2 * ((t + 1) % 2)) + count) % count

    def peer_subj(t):
        return (me_s + t) % subjects

    def greet(s, k):
        pl.semaphore_signal(barrier, inc=1, device_id=(s, k), device_id_type=MESH)

    def greet_slab(t, carry):
        greet(me_s, peer_slab(t))
        return carry

    lax.fori_loop(0, count - 1, greet_slab, 0)
    for t in range(1, subjects):
        greet(peer_subj(t), me_k)

    @pl.when(has_before)
    def _():
        for t in range(1, subjects):
            greet(peer_subj(t), me_k - 1)

    @pl.when(has_after)
    def _():
        for t in range(1, subjects):
            greet(peer_subj(t), me_k + 1)

    def remote(source, target, send, recv, s, k):
        return pltpu.make_async_remote_copy(
            src_ref=source, dst_ref=target, send_sem=send, recv_sem=recv,
            device_id=(s, k), device_id_type=MESH,
        )

    edge = jnp.zeros((8, LANES), jnp.float32)
    height = u_ref.shape[2]
    u_pad[0:8, :] = edge
    u_pad[8 + height:16 + height, :] = edge
    load_u.wait()

    def pad_rows(at, carry):
        a, z = at // SLAB_Z, at % SLAB_Z
        u_pad[8:8 + height, :] = u_ref[a, z]
        for r in range(subjects):
            first = 7 + r * BRICK
            u_rows[r, a, z] = u_pad[first:first + BRICK + 2, :].astype(jnp.bfloat16)
        return carry

    lax.fori_loop(0, 3 * SLAB_Z, pad_rows, 0)
    for side in range(2):
        for a in range(3):
            for r in range(subjects):
                u_edge[side, r, a] = u_ref[
                    a, side * (SLAB_Z - 1), r * BRICK:(r + 1) * BRICK, :
                ].astype(jnp.bfloat16)

    neighbours = (me_k + count - 1) // count + (2 * count - 2 - me_k) // count
    pl.semaphore_wait(barrier, count - 1 + (subjects - 1) * (1 + neighbours))

    def ask(k):
        return remote(code_ref.at[k], asked.at[me_k], ask_send.at[k], ask_recv.at[me_k], me_s, k)

    def ask_from(k):
        return remote(code_ref.at[k], asked.at[k], ask_send.at[k], ask_recv.at[k], me_s, k)

    def start_ask(t, carry):
        ask(peer_slab(t)).start()
        return carry

    lax.fori_loop(0, count - 1, start_ask, 0)
    asked[me_k] = code_ref[me_k]

    def u_block(r):
        return remote(u_rows.at[r], u_all.at[me_s], u_send.at[r], u_recv.at[me_s], r, me_k)

    def u_block_from(s):
        return remote(u_rows.at[s], u_all.at[s], u_send.at[s], u_recv.at[s], s, me_k)

    def u_before(r, s):
        return remote(
            u_edge.at[0, r], u_rim.at[s, 1], up_send.at[r], up_recv.at[s], r, me_k - 1
        )

    def u_after(r, s):
        return remote(
            u_edge.at[1, r], u_rim.at[s, 0], down_send.at[r], down_recv.at[s], r, me_k + 1
        )

    for t in range(1, subjects):
        u_block(peer_subj(t)).start()

    @pl.when(has_before)
    def _():
        for t in range(subjects):
            u_before(peer_subj(t), me_s).start()

    @pl.when(has_after)
    def _():
        for t in range(subjects):
            u_after(peer_subj(t), me_s).start()

    def keep_u(at, carry):
        a, z = at // SLAB_Z, at % SLAB_Z
        u_all[me_s, a, z] = u_rows[me_s, a, z]
        return carry

    lax.fori_loop(0, 3 * SLAB_Z, keep_u, 0)
    rim = jnp.zeros((BRICK, LANES), jnp.bfloat16)

    @pl.when(me_k == 0)
    def _():
        for s in range(subjects):
            for a in range(3):
                u_rim[s, 0, a] = rim

    @pl.when(me_k == count - 1)
    def _():
        for s in range(subjects):
            for a in range(3):
                u_rim[s, 1, a] = rim

    load_bricks.wait()
    relayout_bricks(brick_ref, rows_ref)
    for j in range(4):
        rows_half[:, j * LANES:(j + 1) * LANES] = rows_ref[j].astype(jnp.bfloat16)
    select = selection()

    def wait_ask(t, carry):
        ask_from(peer_slab(t)).wait_recv()
        return carry

    lax.fori_loop(0, count - 1, wait_ask, 0)
    def crop(k, target):
        value = crop_rows(asked[k], capacity, rows_half[...], select).astype(jnp.bfloat16)
        for part in range(PARTS):
            target[part, k] = value[part * capacity * PART_ROWS:(part + 1) * capacity * PART_ROWS]

    def give(k, part):
        return remote(
            crops.at[part, k], arrived.at[part, me_k],
            crop_send.at[part, k], crop_recv.at[part, me_k], me_s, k,
        )

    def take(k, part):
        return remote(
            crops.at[part, k], arrived.at[part, k],
            crop_send.at[part, k], crop_recv.at[part, k], me_s, k,
        )

    def crop_and_give(t, carry):
        reader = peer_slab(t)
        crop(reader, crops)
        give(reader, 0).start()
        return carry

    lax.fori_loop(0, count - 1, crop_and_give, 0)

    for part in range(1, PARTS):
        def give_part(t, carry):
            give(peer_slab(t), part).start()
            return carry

        lax.fori_loop(0, count - 1, give_part, 0)

    crop(me_k, arrived)
    depth = count * capacity * PART_ROWS

    def make_hits(row, carry):
        hits[row] = placing_hits(slot_ref, row, depth)
        return carry

    lax.fori_loop(0, subjects, make_hits, 0)

    for t in range(1, subjects):
        u_block_from(peer_subj(t)).wait_recv()

    @pl.when(has_before)
    def _():
        for t in range(subjects):
            u_after(peer_subj(t), peer_subj(t)).wait_recv()

    @pl.when(has_after)
    def _():
        for t in range(subjects):
            u_before(peer_subj(t), peer_subj(t)).wait_recv()

    def rotate(s, carry):
        for z in range(SLAB_Z):
            layers = [
                [u_all[s, a, near].astype(jnp.float32) if 0 <= near < SLAB_Z else None for a in range(3)]
                for near in (z - 1, z, z + 1)
            ]
            beside = [
                [
                    u_rim[s, side, a].astype(jnp.float32)
                    if layers[2 * side][a] is None
                    else layers[2 * side][a][1:BRICK + 1]
                    for a in range(3)
                ]
                for side in range(2)
            ]
            rotation = rotation_at(layers[1], beside[0], beside[1])
            for a in range(3):
                for b in range(3):
                    rotations[s, z, a * 3 + b] = rotation[a][b]
        return carry

    lax.fori_loop(0, subjects, rotate, 0)

    def share(r, part):
        return remote(
            placed.at[r, part], fields.at[me_s, part],
            field_send.at[part, r], field_recv.at[part, me_s], r, me_k,
        )

    def shared_from(s, part):
        return remote(
            placed.at[s, part], fields.at[s, part],
            field_send.at[part, s], field_recv.at[part, s], s, me_k,
        )

    for part in range(PARTS):
        def collect(t, carry):
            take(peer_slab(t), part).wait_recv()
            return carry

        lax.fori_loop(0, count - 1, collect, 0)
        windows = arrived[part].reshape(depth, FLAT)
        for t in range(1, subjects):
            r = peer_subj(t)
            placed[r, part] = place_row(hits[r], windows)
            share(r, part).start()
        fields[me_s, part] = place_row(hits[me_s], windows)

    def add_subject(t, first):
        s = peer_subj(t)

        def step(z, carry):
            rotation = [[rotations[s, z, a * 3 + b] for b in range(3)] for a in range(3)]
            tensor = [
                fields[s, c // 2, z * 2 + c % 2].astype(jnp.float32) * (1.0 / subjects)
                for c in range(COMP)
            ]
            rotated = reorient(tensor, rotation)
            for c in range(COMP):
                out_ref[c, z] = rotated[c] if first else out_ref[c, z] + rotated[c]
            return carry

        lax.fori_loop(0, SLAB_Z, step, 0)

    add_subject(0, True)
    for t in range(1, subjects):
        for part in range(PARTS):
            shared_from(peer_subj(t), part).wait_recv()
        add_subject(t, False)

    def finish(t, carry):
        k = peer_slab(t)
        ask(k).wait_send()
        for part in range(PARTS):
            give(k, part).wait_send()
        return carry

    lax.fori_loop(0, count - 1, finish, 0)
    for t in range(1, subjects):
        u_block(peer_subj(t)).wait_send()
        for part in range(PARTS):
            share(peer_subj(t), part).wait_send()

    @pl.when(has_before)
    def _():
        for t in range(subjects):
            u_before(peer_subj(t), me_s).wait_send()

    @pl.when(has_after)
    def _():
        for t in range(subjects):
            u_after(peer_subj(t), me_s).wait_send()


MESH = pl.DeviceIdType.MESH
VMEM_SPEC = pl.BlockSpec(memory_space=pltpu.VMEM)
HBM_SPEC = pl.BlockSpec(memory_space=pl.ANY)
SMEM_SPEC = pl.BlockSpec(memory_space=pltpu.SMEM)


def slot_tables(brick_ids, brick_offsets, held, slab_count, capacity):
    wanted = brick_ids[0]
    pieces = wanted.shape[0]
    owner, local = wanted // held, wanted % held
    positions = jnp.arange(pieces, dtype=jnp.int32)
    earlier = (owner[:, None] == owner[None, :]) & (positions[None, :] < positions[:, None])
    slot_of = owner * capacity + jnp.sum(earlier.astype(jnp.int32), axis=1)
    start_z = brick_offsets[0, 0] + lax.axis_index("slab") % ZQ * SLAB_Z
    shift = brick_offsets[0, 1] * EDGE + brick_offsets[0, 2]
    code = (local * BRICK_ROWS + start_z * COMP) * LANES + shift
    hits = slot_of[:, None] == jnp.arange(slab_count * capacity, dtype=jnp.int32)[None, :]
    return slot_of, jnp.sum(jnp.where(hits, code[:, None], 0), axis=0)


def shards(source_bricks, brick_ids, brick_offsets, deformation):
    slab_count, subjects = lax.axis_size("slab"), lax.axis_size("subj")
    pieces = brick_ids.shape[1]
    held = source_bricks.shape[1]
    capacity = max(2, 3 * pieces // (2 * slab_count))
    part_rows = capacity * PART_ROWS
    slot_of, code = slot_tables(brick_ids, brick_offsets, held, slab_count, capacity)
    code = jnp.pad(code.reshape(slab_count, 1, capacity), ((0, 0), (0, 0), (0, LANES - capacity)))
    bf16, f32, dma = jnp.bfloat16, jnp.float32, pltpu.SemaphoreType.DMA
    per_slab, per_subject = dma((slab_count,)), dma((subjects,))
    return pl.pallas_call(
        warp_kernel,
        out_shape=jax.ShapeDtypeStruct((COMP, SLAB_Z, BRICK, LANES), f32),
        in_specs=[VMEM_SPEC, SMEM_SPEC, HBM_SPEC, HBM_SPEC],
        out_specs=VMEM_SPEC,
        scratch_shapes=[
            pltpu.VMEM(source_bricks.shape[1:], bf16),
            pltpu.VMEM(deformation.shape[1:], f32),
            pltpu.VMEM((slab_count, 1, LANES), jnp.int32),
            pltpu.VMEM((4, held * BRICK_ROWS, LANES), f32),
            pltpu.VMEM((held * BRICK_ROWS, 4 * LANES), bf16),
            pltpu.VMEM((PARTS, slab_count, part_rows, FLAT), bf16),
            pltpu.VMEM((PARTS, slab_count, part_rows, FLAT), bf16),
            pltpu.VMEM((subjects, LANES // BRICK * PART_ROWS, slab_count * part_rows), bf16),
            pltpu.VMEM((deformation.shape[3] + 16, LANES), f32),
            pltpu.VMEM((subjects, 3, SLAB_Z, BRICK + 2, LANES), bf16),
            pltpu.VMEM((2, subjects, 3, BRICK, LANES), bf16),
            pltpu.VMEM((subjects, 3, SLAB_Z, BRICK + 2, LANES), bf16),
            pltpu.VMEM((subjects, 2, 3, BRICK, LANES), bf16),
            pltpu.VMEM((subjects, SLAB_Z, 9, BRICK, LANES), f32),
            pltpu.VMEM((subjects, PARTS, PART_ROWS, BRICK, LANES), bf16),
            pltpu.VMEM((subjects, PARTS, PART_ROWS, BRICK, LANES), bf16),
            dma((2,)),
            per_slab, per_slab, dma((PARTS, slab_count)), dma((PARTS, slab_count)),
            per_subject, per_subject, per_subject, per_subject,
            per_subject, per_subject, dma((PARTS, subjects)), dma((PARTS, subjects)),
        ],
        compiler_params=pltpu.CompilerParams(
            vmem_limit_bytes=48 << 20, collective_id=0, has_side_effects=True
        ),
    )(code, slot_of, source_bricks, deformation)


def solution(mesh):
    in_specs = (
        P("subj", "slab", None),
        P("subj", "slab"),
        P("subj", None, "slab"),
        P("subj", None, "slab", None, None),
    )
    out_specs = P(None, "slab", "subj", None)
    return jax.shard_map(shards, mesh=mesh, in_specs=in_specs, out_specs=out_specs, check_vma=False)
```

```python
import jax
import jax.numpy as jnp
from jax import lax
from jax.experimental import pallas as pl
from jax.experimental.pallas import tpu as pltpu
from jax.sharding import PartitionSpec as P

COMP = 6
BRICK = 16
PAD = 2
EDGE = BRICK + 2 * PAD
ZQ = 4
NEWTON = 2
SLAB_Z = 4
LANES = 128
ROWS = COMP * SLAB_Z
BRICK_ROWS = COMP * EDGE
PARTS = COMP // 2
PART_ROWS = 2 * SLAB_Z
SPAN = 384
FLAT = BRICK * BRICK


def relayout_bricks(x_ref, rows_ref):
    held = x_ref.shape[0]
    lane = lax.broadcasted_iota(jnp.int32, (held, LANES), 1)
    group_lanes = 8 * EDGE * EDGE

    def step(group, carry):
        for m in range(8):
            cz = group * 8 + m
            row = cz % EDGE * (held * COMP) + cz // EDGE
            shift = 16 * m
            tiles = []
            for j in range(4):
                first = pl.multiple_of(group * group_lanes + (3 * m + j) * LANES, LANES)
                tile = x_ref[:, pl.ds(first, LANES)].astype(jnp.float32)
                tiles.append(pltpu.roll(tile, LANES - shift, 1) if shift else tile)
            for j in range(4):
                value = tiles[j]
                if shift and j < 3:
                    value = jnp.where(lane < LANES - shift, tiles[j], tiles[j + 1])
                rows_ref[j, pl.ds(row, held, stride=COMP), :] = value
        return carry

    lax.fori_loop(0, BRICK_ROWS // 8, step, 0)


def selection():
    source = lax.broadcasted_iota(jnp.int32, (SPAN, FLAT), 0)
    target = lax.broadcasted_iota(jnp.int32, (SPAN, FLAT), 1)
    return (source == target // BRICK * EDGE + target % BRICK).astype(jnp.float32).astype(jnp.bfloat16)


def crop_rows(codes, capacity, rows, select):
    depth = rows.shape[0]
    layer = depth // (SLAB_Z + 2 * PAD)
    row = lax.broadcasted_iota(jnp.int32, (PART_ROWS, depth), 0)
    offset = lax.broadcasted_iota(jnp.int32, (PART_ROWS, depth), 1) - (row // 2 * layer + row % 2)
    hits, shifts = [], []
    for slot in range(capacity):
        code = codes[:, slot:slot + 1]
        start = lax.shift_right_logical(code, jnp.full(code.shape, 7, jnp.int32))
        hits.append(offset - jnp.broadcast_to(start, (PART_ROWS, depth)))
        shifts.append(jnp.broadcast_to(code & (LANES - 1), (PART_ROWS, LANES)))
    hit = jnp.concatenate(
        [(hits[slot] == 2 * part).astype(jnp.float32) for part in range(PARTS) for slot in range(capacity)],
        axis=0,
    ).astype(jnp.bfloat16)
    shift = jnp.concatenate(shifts * PARTS, axis=0)
    found = jnp.dot(hit, rows, preferred_element_type=jnp.float32)
    tiles = [found[:, j * LANES:(j + 1) * LANES] for j in range(4)]
    for bit in (1, 2, 4, 8, 16, 32, 64):
        taken = (shift & bit) != 0
        tiles = [jnp.where(taken, pltpu.roll(tile, LANES - bit, 1), tile) for tile in tiles]
    inside = lax.broadcasted_iota(jnp.int32, shift.shape, 1) + shift < LANES
    shifted = [jnp.where(inside, tiles[j], tiles[j + 1]).astype(jnp.bfloat16) for j in range(3)]
    return jnp.dot(jnp.concatenate(shifted, axis=1), select, preferred_element_type=jnp.float32)


def swap_groups(value):
    sub = lax.broadcasted_iota(jnp.int32, value.shape, 1)
    group = lax.broadcasted_iota(jnp.int32, value.shape, 2) // BRICK
    for bit in (1, 2, 4):
        from_below = pltpu.roll(pltpu.roll(value, 8 - bit, 1), BRICK * bit, 2)
        if bit == 4:
            from_above = from_below
        else:
            from_above = pltpu.roll(pltpu.roll(value, bit, 1), LANES - BRICK * bit, 2)
        low = (sub & bit) == 0
        same = (sub & bit) == (group & bit)
        value = jnp.where(same, value, jnp.where(low, from_below, from_above))
    return value


def placing_hits(slot_ref, row, depth):
    across = LANES // BRICK
    sub = lax.broadcasted_iota(jnp.int32, (across, depth), 0)
    base = jnp.zeros((across, depth), jnp.int32)
    for j in range(across):
        base = jnp.where(sub == j, slot_ref[row * across + j] * PART_ROWS, base)
    offset = lax.broadcasted_iota(jnp.int32, (across, depth), 1) - base
    return jnp.concatenate(
        [(offset == n).astype(jnp.float32) for n in range(PART_ROWS)], axis=0
    ).astype(jnp.bfloat16)


def place_row(hit, windows):
    pieces = jnp.dot(hit, windows, preferred_element_type=jnp.float32)
    halves = [
        swap_groups(pieces[:, h * LANES:(h + 1) * LANES].reshape(PART_ROWS, 8, LANES))
        for h in range(2)
    ]
    return jnp.concatenate(halves, axis=1).astype(jnp.bfloat16)


def polar_factor(matrix):
    for newton_step in range(NEWTON):
        cofactor = [
            [
                matrix[(a + 1) % 3][(b + 1) % 3] * matrix[(a + 2) % 3][(b + 2) % 3]
                - matrix[(a + 1) % 3][(b + 2) % 3] * matrix[(a + 2) % 3][(b + 1) % 3]
                for b in range(3)
            ]
            for a in range(3)
        ]
        determinant = (
            matrix[0][0] * cofactor[0][0]
            + matrix[0][1] * cofactor[0][1]
            + matrix[0][2] * cofactor[0][2]
        )
        scaling = 0.5 / determinant
        matrix = [
            [0.5 * matrix[a][b] + cofactor[a][b] * scaling for b in range(3)] for a in range(3)
        ]
    return matrix


def reorient(components, rotation):
    tensor_rows = [
        [components[0], components[3], components[4]],
        [components[3], components[1], components[5]],
        [components[4], components[5], components[2]],
    ]
    left_side = [
        [
            rotation[a][0] * tensor_rows[0][b]
            + rotation[a][1] * tensor_rows[1][b]
            + rotation[a][2] * tensor_rows[2][b]
            for b in range(3)
        ]
        for a in range(3)
    ]
    pair_list = ((0, 0), (1, 1), (2, 2), (0, 1), (0, 2), (1, 2))
    return [
        left_side[a][0] * rotation[b][0]
        + left_side[a][1] * rotation[b][1]
        + left_side[a][2] * rotation[b][2]
        for a, b in pair_list
    ]


def rotation_at(centre, before, after):
    lane = lax.broadcasted_iota(jnp.int32, (BRICK, LANES), 1)
    matrix = []
    for a in range(3):
        here = centre[a][1:BRICK + 1]
        along_z = (after[a] - before[a]) * 0.5
        along_y = (centre[a][2:BRICK + 2] - centre[a][0:BRICK]) * 0.5
        later = jnp.where(lane == LANES - 1, 0.0, pltpu.roll(here, LANES - 1, 1))
        earlier = jnp.where(lane == 0, 0.0, pltpu.roll(here, 1, 1))
        gradients = [along_z, along_y, (later - earlier) * 0.5]
        gradients[a] = gradients[a] + 1.0
        matrix.append(gradients)
    return polar_factor(matrix)


def warp_kernel(
    code_ref, slot_ref, brick_hbm, u_hbm, out_ref,
    brick_ref, u_ref, asked, rows_ref, rows_half, crops, arrived, hits,
    u_pad, u_rows, u_edge, u_all, u_rim, rotations, placed, fields, load_sem,
    ask_send, ask_recv, crop_send, crop_recv, u_send, u_recv, up_send, up_recv,
    down_send, down_recv, field_send, field_recv,
):
    count, subjects = arrived.shape[1], fields.shape[0]
    capacity = arrived.shape[2] // PART_ROWS
    load_u = pltpu.make_async_copy(u_hbm.at[0], u_ref, load_sem.at[0])
    load_u.start()
    load_bricks = pltpu.make_async_copy(brick_hbm.at[0], brick_ref, load_sem.at[1])
    load_bricks.start()
    me_s, me_k = lax.axis_index("subj"), lax.axis_index("slab")
    barrier = pltpu.get_barrier_semaphore()
    has_before, has_after = me_k > 0, me_k < count - 1

    def peer_slab(t):
        turn = (t + 1) // 2
        return (me_k + count // 2 + turn * (1 - 2 * ((t + 1) % 2)) + count) % count

    def peer_subj(t):
        return (me_s + t) % subjects

    def greet(s, k):
        pl.semaphore_signal(barrier, inc=1, device_id=(s, k), device_id_type=MESH)

    def greet_slab(t, carry):
        greet(me_s, peer_slab(t))
        return carry

    lax.fori_loop(0, count - 1, greet_slab, 0)
    for t in range(1, subjects):
        greet(peer_subj(t), me_k)

    @pl.when(has_before)
    def _():
        for t in range(1, subjects):
            greet(peer_subj(t), me_k - 1)

    @pl.when(has_after)
    def _():
        for t in range(1, subjects):
            greet(peer_subj(t), me_k + 1)

    def remote(source, target, send, recv, s, k):
        return pltpu.make_async_remote_copy(
            src_ref=source, dst_ref=target, send_sem=send, recv_sem=recv,
            device_id=(s, k), device_id_type=MESH,
        )

    edge = jnp.zeros((8, LANES), jnp.float32)
    height = u_ref.shape[2]
    u_pad[0:8, :] = edge
    u_pad[8 + height:16 + height, :] = edge
    load_u.wait()

    def pad_rows(at, carry):
        a, z = at // SLAB_Z, at % SLAB_Z
        u_pad[8:8 + height, :] = u_ref[a, z]
        for r in range(subjects):
            first = 7 + r * BRICK
            u_rows[r, a, z] = u_pad[first:first + BRICK + 2, :].astype(jnp.bfloat16)
        return carry

    lax.fori_loop(0, 3 * SLAB_Z, pad_rows, 0)
    for side in range(2):
        for a in range(3):
            for r in range(subjects):
                u_edge[side, r, a] = u_ref[
                    a, side * (SLAB_Z - 1), r * BRICK:(r + 1) * BRICK, :
                ].astype(jnp.bfloat16)

    neighbours = (me_k + count - 1) // count + (2 * count - 2 - me_k) // count
    pl.semaphore_wait(barrier, count - 1 + (subjects - 1) * (1 + neighbours))

    def ask(k):
        return remote(code_ref.at[k], asked.at[me_k], ask_send.at[k], ask_recv.at[me_k], me_s, k)

    def ask_from(k):
        return remote(code_ref.at[k], asked.at[k], ask_send.at[k], ask_recv.at[k], me_s, k)

    def start_ask(t, carry):
        ask(peer_slab(t)).start()
        return carry

    lax.fori_loop(0, count - 1, start_ask, 0)
    asked[me_k] = code_ref[me_k]

    def u_block(r):
        return remote(u_rows.at[r], u_all.at[me_s], u_send.at[r], u_recv.at[me_s], r, me_k)

    def u_block_from(s):
        return remote(u_rows.at[s], u_all.at[s], u_send.at[s], u_recv.at[s], s, me_k)

    def u_before(r, s):
        return remote(
            u_edge.at[0, r], u_rim.at[s, 1], up_send.at[r], up_recv.at[s], r, me_k - 1
        )

    def u_after(r, s):
        return remote(
            u_edge.at[1, r], u_rim.at[s, 0], down_send.at[r], down_recv.at[s], r, me_k + 1
        )

    for t in range(1, subjects):
        u_block(peer_subj(t)).start()

    @pl.when(has_before)
    def _():
        for t in range(subjects):
            u_before(peer_subj(t), me_s).start()

    @pl.when(has_after)
    def _():
        for t in range(subjects):
            u_after(peer_subj(t), me_s).start()

    def keep_u(at, carry):
        a, z = at // SLAB_Z, at % SLAB_Z
        u_all[me_s, a, z] = u_rows[me_s, a, z]
        return carry

    lax.fori_loop(0, 3 * SLAB_Z, keep_u, 0)
    rim = jnp.zeros((BRICK, LANES), jnp.bfloat16)

    @pl.when(me_k == 0)
    def _():
        for s in range(subjects):
            for a in range(3):
                u_rim[s, 0, a] = rim

    @pl.when(me_k == count - 1)
    def _():
        for s in range(subjects):
            for a in range(3):
                u_rim[s, 1, a] = rim

    load_bricks.wait()
    relayout_bricks(brick_ref, rows_ref)
    for j in range(4):
        rows_half[:, j * LANES:(j + 1) * LANES] = rows_ref[j].astype(jnp.bfloat16)
    select = selection()

    def wait_ask(t, carry):
        ask_from(peer_slab(t)).wait_recv()
        return carry

    lax.fori_loop(0, count - 1, wait_ask, 0)
    layer = brick_ref.shape[0] * COMP

    def crop(k, target):
        first = pl.multiple_of(k % ZQ * SLAB_Z * layer, 16)
        rows = rows_half[pl.ds(first, (SLAB_Z + 2 * PAD) * layer), :]
        value = crop_rows(asked[k], capacity, rows, select).astype(jnp.bfloat16)
        for part in range(PARTS):
            target[part, k] = value[part * capacity * PART_ROWS:(part + 1) * capacity * PART_ROWS]

    def give(k, part):
        return remote(
            crops.at[part, k], arrived.at[part, me_k],
            crop_send.at[part, k], crop_recv.at[part, me_k], me_s, k,
        )

    def take(k, part):
        return remote(
            crops.at[part, k], arrived.at[part, k],
            crop_send.at[part, k], crop_recv.at[part, k], me_s, k,
        )

    def crop_and_give(t, carry):
        reader = peer_slab(t)
        crop(reader, crops)
        give(reader, 0).start()
        return carry

    lax.fori_loop(0, count - 1, crop_and_give, 0)

    for part in range(1, PARTS):
        def give_part(t, carry):
            give(peer_slab(t), part).start()
            return carry

        lax.fori_loop(0, count - 1, give_part, 0)

    crop(me_k, arrived)
    depth = count * capacity * PART_ROWS

    def make_hits(row, carry):
        hits[row] = placing_hits(slot_ref, row, depth)
        return carry

    lax.fori_loop(0, subjects, make_hits, 0)

    for t in range(1, subjects):
        u_block_from(peer_subj(t)).wait_recv()

    @pl.when(has_before)
    def _():
        for t in range(subjects):
            u_after(peer_subj(t), peer_subj(t)).wait_recv()

    @pl.when(has_after)
    def _():
        for t in range(subjects):
            u_before(peer_subj(t), peer_subj(t)).wait_recv()

    def rotate(s, carry):
        for z in range(SLAB_Z):
            layers = [
                [u_all[s, a, near].astype(jnp.float32) if 0 <= near < SLAB_Z else None for a in range(3)]
                for near in (z - 1, z, z + 1)
            ]
            beside = [
                [
                    u_rim[s, side, a].astype(jnp.float32)
                    if layers[2 * side][a] is None
                    else layers[2 * side][a][1:BRICK + 1]
                    for a in range(3)
                ]
                for side in range(2)
            ]
            rotation = rotation_at(layers[1], beside[0], beside[1])
            for a in range(3):
                for b in range(3):
                    rotations[s, z, a * 3 + b] = rotation[a][b]
        return carry

    lax.fori_loop(0, subjects, rotate, 0)

    def share(r, part):
        return remote(
            placed.at[r, part], fields.at[me_s, part],
            field_send.at[part, r], field_recv.at[part, me_s], r, me_k,
        )

    def shared_from(s, part):
        return remote(
            placed.at[s, part], fields.at[s, part],
            field_send.at[part, s], field_recv.at[part, s], s, me_k,
        )

    for part in range(PARTS):
        def collect(t, carry):
            take(peer_slab(t), part).wait_recv()
            return carry

        lax.fori_loop(0, count - 1, collect, 0)
        windows = arrived[part].reshape(depth, FLAT)
        for t in range(1, subjects):
            r = peer_subj(t)
            placed[r, part] = place_row(hits[r], windows)
            share(r, part).start()
        fields[me_s, part] = place_row(hits[me_s], windows)

    def add_subject(t, first):
        s = peer_subj(t)

        def step(z, carry):
            rotation = [[rotations[s, z, a * 3 + b] for b in range(3)] for a in range(3)]
            tensor = [
                fields[s, c // 2, z * 2 + c % 2].astype(jnp.float32) * (1.0 / subjects)
                for c in range(COMP)
            ]
            rotated = reorient(tensor, rotation)
            for c in range(COMP):
                out_ref[c, z] = rotated[c] if first else out_ref[c, z] + rotated[c]
            return carry

        lax.fori_loop(0, SLAB_Z, step, 0)

    add_subject(0, True)
    for t in range(1, subjects):
        for part in range(PARTS):
            shared_from(peer_subj(t), part).wait_recv()
        add_subject(t, False)

    def finish(t, carry):
        k = peer_slab(t)
        ask(k).wait_send()
        for part in range(PARTS):
            give(k, part).wait_send()
        return carry

    lax.fori_loop(0, count - 1, finish, 0)
    for t in range(1, subjects):
        u_block(peer_subj(t)).wait_send()
        for part in range(PARTS):
            share(peer_subj(t), part).wait_send()

    @pl.when(has_before)
    def _():
        for t in range(subjects):
            u_before(peer_subj(t), me_s).wait_send()

    @pl.when(has_after)
    def _():
        for t in range(subjects):
            u_after(peer_subj(t), me_s).wait_send()


MESH = pl.DeviceIdType.MESH
VMEM_SPEC = pl.BlockSpec(memory_space=pltpu.VMEM)
HBM_SPEC = pl.BlockSpec(memory_space=pltpu.HBM)
SMEM_SPEC = pl.BlockSpec(memory_space=pltpu.SMEM)


def slot_tables(brick_ids, brick_offsets, held, slab_count, capacity):
    wanted = brick_ids[0]
    pieces = wanted.shape[0]
    owner, local = wanted // held, wanted % held
    positions = jnp.arange(pieces, dtype=jnp.int32)
    earlier = (owner[:, None] == owner[None, :]) & (positions[None, :] < positions[:, None])
    slot_of = owner * capacity + jnp.sum(earlier.astype(jnp.int32), axis=1)
    shift = brick_offsets[0, 1] * EDGE + brick_offsets[0, 2]
    code = (local + brick_offsets[0, 0] * held) * COMP * LANES + shift
    hits = slot_of[:, None] == jnp.arange(slab_count * capacity, dtype=jnp.int32)[None, :]
    return slot_of, jnp.sum(jnp.where(hits, code[:, None], 0), axis=0)


def shards(source_bricks, brick_ids, brick_offsets, deformation):
    slab_count, subjects = lax.axis_size("slab"), lax.axis_size("subj")
    pieces = brick_ids.shape[1]
    held = source_bricks.shape[1]
    capacity = max(2, 3 * pieces // (2 * slab_count))
    part_rows = capacity * PART_ROWS
    slot_of, code = slot_tables(brick_ids, brick_offsets, held, slab_count, capacity)
    code = jnp.pad(code.reshape(slab_count, 1, capacity), ((0, 0), (0, 0), (0, LANES - capacity)))
    bf16, f32, dma = jnp.bfloat16, jnp.float32, pltpu.SemaphoreType.DMA
    per_slab, per_subject = dma((slab_count,)), dma((subjects,))
    return pl.pallas_call(
        warp_kernel,
        out_shape=jax.ShapeDtypeStruct((COMP, SLAB_Z, BRICK, LANES), f32),
        in_specs=[VMEM_SPEC, SMEM_SPEC, HBM_SPEC, HBM_SPEC],
        out_specs=VMEM_SPEC,
        scratch_shapes=[
            pltpu.VMEM(source_bricks.shape[1:], bf16),
            pltpu.VMEM(deformation.shape[1:], f32),
            pltpu.VMEM((slab_count, 1, LANES), jnp.int32),
            pltpu.VMEM((4, held * BRICK_ROWS, LANES), f32),
            pltpu.VMEM((held * BRICK_ROWS, 4 * LANES), bf16),
            pltpu.VMEM((PARTS, slab_count, part_rows, FLAT), bf16),
            pltpu.VMEM((PARTS, slab_count, part_rows, FLAT), bf16),
            pltpu.VMEM((subjects, LANES // BRICK * PART_ROWS, slab_count * part_rows), bf16),
            pltpu.VMEM((deformation.shape[3] + 16, LANES), f32),
            pltpu.VMEM((subjects, 3, SLAB_Z, BRICK + 2, LANES), bf16),
            pltpu.VMEM((2, subjects, 3, BRICK, LANES), bf16),
            pltpu.VMEM((subjects, 3, SLAB_Z, BRICK + 2, LANES), bf16),
            pltpu.VMEM((subjects, 2, 3, BRICK, LANES), bf16),
            pltpu.VMEM((subjects, SLAB_Z, 9, BRICK, LANES), f32),
            pltpu.VMEM((subjects, PARTS, PART_ROWS, BRICK, LANES), bf16),
            pltpu.VMEM((subjects, PARTS, PART_ROWS, BRICK, LANES), bf16),
            dma((2,)),
            per_slab, per_slab, dma((PARTS, slab_count)), dma((PARTS, slab_count)),
            per_subject, per_subject, per_subject, per_subject,
            per_subject, per_subject, dma((PARTS, subjects)), dma((PARTS, subjects)),
        ],
        compiler_params=pltpu.CompilerParams(
            vmem_limit_bytes=48 << 20, collective_id=0, has_side_effects=True
        ),
    )(code, slot_of, source_bricks, deformation)


def solution(mesh):
    in_specs = (
        P("subj", "slab", None),
        P("subj", "slab"),
        P("subj", None, "slab"),
        P("subj", None, "slab", None, None),
    )
    out_specs = P(None, "slab", "subj", None)
    return jax.shard_map(shards, mesh=mesh, in_specs=in_specs, out_specs=out_specs, check_vma=False)
```

```python
import jax
import jax.numpy as jnp
from jax import lax
from jax.experimental import pallas as pl
from jax.experimental.pallas import tpu as pltpu
from jax.sharding import PartitionSpec as P

COMP = 6
BRICK = 16
PAD = 2
EDGE = BRICK + 2 * PAD
ZQ = 4
NEWTON = 2
SLAB_Z = 4
LANES = 128
ROWS = COMP * SLAB_Z
BRICK_ROWS = COMP * EDGE
PARTS = 1
PART_COMP = COMP // PARTS
PART_ROWS = PART_COMP * SLAB_Z
SPAN = 384
FLAT = BRICK * BRICK


def relayout_bricks(x_ref, rows_ref):
    held = x_ref.shape[0]
    lane = lax.broadcasted_iota(jnp.int32, (held, LANES), 1)
    group_lanes = 8 * EDGE * EDGE

    def step(group, carry):
        for m in range(8):
            cz = group * 8 + m
            row = cz % EDGE * (held * COMP) + cz // EDGE
            shift = 16 * m
            tiles = []
            for j in range(4):
                first = pl.multiple_of(group * group_lanes + (3 * m + j) * LANES, LANES)
                tile = x_ref[:, pl.ds(first, LANES)].astype(jnp.float32)
                tiles.append(pltpu.roll(tile, LANES - shift, 1) if shift else tile)
            for j in range(4):
                value = tiles[j]
                if shift and j < 3:
                    value = jnp.where(lane < LANES - shift, tiles[j], tiles[j + 1])
                rows_ref[j, pl.ds(row, held, stride=COMP), :] = value
        return carry

    lax.fori_loop(0, BRICK_ROWS // 8, step, 0)


def selection():
    source = lax.broadcasted_iota(jnp.int32, (SPAN, FLAT), 0)
    target = lax.broadcasted_iota(jnp.int32, (SPAN, FLAT), 1)
    return (source == target // BRICK * EDGE + target % BRICK).astype(jnp.float32).astype(jnp.bfloat16)


def crop_rows(codes, capacity, rows, select):
    depth = rows.shape[0]
    layer = depth // (SLAB_Z + 2 * PAD)
    row = lax.broadcasted_iota(jnp.int32, (PART_ROWS, depth), 0)
    offset = lax.broadcasted_iota(jnp.int32, (PART_ROWS, depth), 1) - (row // PART_COMP * layer + row % PART_COMP)
    hits, shifts = [], []
    for slot in range(capacity):
        code = codes[:, slot:slot + 1]
        start = lax.shift_right_logical(code, jnp.full(code.shape, 7, jnp.int32))
        hits.append(offset - jnp.broadcast_to(start, (PART_ROWS, depth)))
        shifts.append(jnp.broadcast_to(code & (LANES - 1), (PART_ROWS, LANES)))
    hit = jnp.concatenate(
        [(hits[slot] == PART_COMP * part).astype(jnp.float32) for part in range(PARTS) for slot in range(capacity)],
        axis=0,
    ).astype(jnp.bfloat16)
    shift = jnp.concatenate(shifts * PARTS, axis=0)
    found = jnp.dot(hit, rows, preferred_element_type=jnp.float32)
    tiles = [found[:, j * LANES:(j + 1) * LANES] for j in range(4)]
    for bit in (1, 2, 4, 8, 16, 32, 64):
        taken = (shift & bit) != 0
        tiles = [jnp.where(taken, pltpu.roll(tile, LANES - bit, 1), tile) for tile in tiles]
    inside = lax.broadcasted_iota(jnp.int32, shift.shape, 1) + shift < LANES
    shifted = [jnp.where(inside, tiles[j], tiles[j + 1]).astype(jnp.bfloat16) for j in range(3)]
    return jnp.dot(jnp.concatenate(shifted, axis=1), select, preferred_element_type=jnp.float32)


def swap_groups(value):
    sub = lax.broadcasted_iota(jnp.int32, value.shape, 1)
    group = lax.broadcasted_iota(jnp.int32, value.shape, 2) // BRICK
    for bit in (1, 2, 4):
        from_below = pltpu.roll(pltpu.roll(value, 8 - bit, 1), BRICK * bit, 2)
        if bit == 4:
            from_above = from_below
        else:
            from_above = pltpu.roll(pltpu.roll(value, bit, 1), LANES - BRICK * bit, 2)
        low = (sub & bit) == 0
        same = (sub & bit) == (group & bit)
        value = jnp.where(same, value, jnp.where(low, from_below, from_above))
    return value


def placing_hits(slot_ref, row, depth):
    across = LANES // BRICK
    sub = lax.broadcasted_iota(jnp.int32, (across, depth), 0)
    base = jnp.zeros((across, depth), jnp.int32)
    for j in range(across):
        base = jnp.where(sub == j, slot_ref[row * across + j] * PART_ROWS, base)
    offset = lax.broadcasted_iota(jnp.int32, (across, depth), 1) - base
    return jnp.concatenate(
        [(offset == n).astype(jnp.float32) for n in range(PART_ROWS)], axis=0
    ).astype(jnp.bfloat16)


def place_row(hit, windows):
    pieces = jnp.dot(hit, windows, preferred_element_type=jnp.float32)
    halves = [
        swap_groups(pieces[:, h * LANES:(h + 1) * LANES].reshape(PART_ROWS, 8, LANES))
        for h in range(2)
    ]
    return jnp.concatenate(halves, axis=1).astype(jnp.bfloat16)


def polar_factor(matrix):
    for newton_step in range(NEWTON):
        cofactor = [
            [
                matrix[(a + 1) % 3][(b + 1) % 3] * matrix[(a + 2) % 3][(b + 2) % 3]
                - matrix[(a + 1) % 3][(b + 2) % 3] * matrix[(a + 2) % 3][(b + 1) % 3]
                for b in range(3)
            ]
            for a in range(3)
        ]
        determinant = (
            matrix[0][0] * cofactor[0][0]
            + matrix[0][1] * cofactor[0][1]
            + matrix[0][2] * cofactor[0][2]
        )
        scaling = 0.5 / determinant
        matrix = [
            [0.5 * matrix[a][b] + cofactor[a][b] * scaling for b in range(3)] for a in range(3)
        ]
    return matrix


def reorient(components, rotation):
    tensor_rows = [
        [components[0], components[3], components[4]],
        [components[3], components[1], components[5]],
        [components[4], components[5], components[2]],
    ]
    left_side = [
        [
            rotation[a][0] * tensor_rows[0][b]
            + rotation[a][1] * tensor_rows[1][b]
            + rotation[a][2] * tensor_rows[2][b]
            for b in range(3)
        ]
        for a in range(3)
    ]
    pair_list = ((0, 0), (1, 1), (2, 2), (0, 1), (0, 2), (1, 2))
    return [
        left_side[a][0] * rotation[b][0]
        + left_side[a][1] * rotation[b][1]
        + left_side[a][2] * rotation[b][2]
        for a, b in pair_list
    ]


def rotation_at(centre, before, after):
    lane = lax.broadcasted_iota(jnp.int32, (BRICK, LANES), 1)
    matrix = []
    for a in range(3):
        here = centre[a][1:BRICK + 1]
        along_z = (after[a] - before[a]) * 0.5
        along_y = (centre[a][2:BRICK + 2] - centre[a][0:BRICK]) * 0.5
        later = jnp.where(lane == LANES - 1, 0.0, pltpu.roll(here, LANES - 1, 1))
        earlier = jnp.where(lane == 0, 0.0, pltpu.roll(here, 1, 1))
        gradients = [along_z, along_y, (later - earlier) * 0.5]
        gradients[a] = gradients[a] + 1.0
        matrix.append(gradients)
    return polar_factor(matrix)


def warp_kernel(
    code_hbm, slot_hbm, brick_hbm, u_hbm, out_ref,
    code_ref, slot_ref, brick_ref, u_ref, asked, rows_ref, rows_half, crops, arrived, hits,
    u_pad, u_rows, u_edge, u_all, u_rim, rotations, placed, fields, load_sem,
    ask_send, ask_recv, crop_send, crop_recv, u_send, u_recv, up_send, up_recv,
    down_send, down_recv, field_send, field_recv,
):
    count, subjects = arrived.shape[1], fields.shape[0]
    capacity = arrived.shape[2] // PART_ROWS
    load_code = pltpu.make_async_copy(code_hbm, code_ref, load_sem.at[2])
    load_code.start()
    load_slot = pltpu.make_async_copy(slot_hbm, slot_ref, load_sem.at[3])
    load_slot.start()
    load_u = pltpu.make_async_copy(u_hbm.at[0], u_ref, load_sem.at[0])
    load_u.start()
    load_bricks = pltpu.make_async_copy(brick_hbm.at[0], brick_ref, load_sem.at[1])
    load_bricks.start()
    me_s, me_k = lax.axis_index("subj"), lax.axis_index("slab")
    barrier = pltpu.get_barrier_semaphore()
    has_before, has_after = me_k > 0, me_k < count - 1

    def peer_slab(t):
        turn = (t + 1) // 2
        return (me_k + count // 2 + turn * (1 - 2 * ((t + 1) % 2)) + count) % count

    def peer_subj(t):
        return (me_s + t) % subjects

    def greet(s, k):
        pl.semaphore_signal(barrier, inc=1, device_id=(s, k), device_id_type=MESH)

    def greet_slab(t, carry):
        greet(me_s, peer_slab(t))
        return carry

    lax.fori_loop(0, count - 1, greet_slab, 0)
    for t in range(1, subjects):
        greet(peer_subj(t), me_k)

    @pl.when(has_before)
    def _():
        for t in range(1, subjects):
            greet(peer_subj(t), me_k - 1)

    @pl.when(has_after)
    def _():
        for t in range(1, subjects):
            greet(peer_subj(t), me_k + 1)

    def remote(source, target, send, recv, s, k):
        return pltpu.make_async_remote_copy(
            src_ref=source, dst_ref=target, send_sem=send, recv_sem=recv,
            device_id=(s, k), device_id_type=MESH,
        )

    edge = jnp.zeros((8, LANES), jnp.float32)
    height = u_ref.shape[2]
    u_pad[0:8, :] = edge
    u_pad[8 + height:16 + height, :] = edge
    load_u.wait()

    def pad_rows(at, carry):
        a, z = at // SLAB_Z, at % SLAB_Z
        u_pad[8:8 + height, :] = u_ref[a, z]
        for r in range(subjects):
            first = 7 + r * BRICK
            u_rows[r, a, z] = u_pad[first:first + BRICK + 2, :].astype(jnp.bfloat16)
        return carry

    lax.fori_loop(0, 3 * SLAB_Z, pad_rows, 0)
    for side in range(2):
        for a in range(3):
            for r in range(subjects):
                u_edge[side, r, a] = u_ref[
                    a, side * (SLAB_Z - 1), r * BRICK:(r + 1) * BRICK, :
                ].astype(jnp.bfloat16)

    neighbours = (me_k + count - 1) // count + (2 * count - 2 - me_k) // count
    pl.semaphore_wait(barrier, count - 1 + (subjects - 1) * (1 + neighbours))

    load_code.wait()

    def ask(k):
        return remote(code_ref.at[k], asked.at[me_k], ask_send.at[k], ask_recv.at[me_k], me_s, k)

    def ask_from(k):
        return remote(code_ref.at[k], asked.at[k], ask_send.at[k], ask_recv.at[k], me_s, k)

    def start_ask(t, carry):
        ask(peer_slab(t)).start()
        return carry

    lax.fori_loop(0, count - 1, start_ask, 0)
    asked[me_k] = code_ref[me_k]

    def u_block(r):
        return remote(u_rows.at[r], u_all.at[me_s], u_send.at[r], u_recv.at[me_s], r, me_k)

    def u_block_from(s):
        return remote(u_rows.at[s], u_all.at[s], u_send.at[s], u_recv.at[s], s, me_k)

    def u_before(r, s):
        return remote(
            u_edge.at[0, r], u_rim.at[s, 1], up_send.at[r], up_recv.at[s], r, me_k - 1
        )

    def u_after(r, s):
        return remote(
            u_edge.at[1, r], u_rim.at[s, 0], down_send.at[r], down_recv.at[s], r, me_k + 1
        )

    for t in range(1, subjects):
        u_block(peer_subj(t)).start()

    @pl.when(has_before)
    def _():
        for t in range(subjects):
            u_before(peer_subj(t), me_s).start()

    @pl.when(has_after)
    def _():
        for t in range(subjects):
            u_after(peer_subj(t), me_s).start()

    def keep_u(at, carry):
        a, z = at // SLAB_Z, at % SLAB_Z
        u_all[me_s, a, z] = u_rows[me_s, a, z]
        return carry

    lax.fori_loop(0, 3 * SLAB_Z, keep_u, 0)
    rim = jnp.zeros((BRICK, LANES), jnp.bfloat16)

    @pl.when(me_k == 0)
    def _():
        for s in range(subjects):
            for a in range(3):
                u_rim[s, 0, a] = rim

    @pl.when(me_k == count - 1)
    def _():
        for s in range(subjects):
            for a in range(3):
                u_rim[s, 1, a] = rim

    load_bricks.wait()
    relayout_bricks(brick_ref, rows_ref)
    for j in range(4):
        rows_half[:, j * LANES:(j + 1) * LANES] = rows_ref[j].astype(jnp.bfloat16)
    select = selection()

    def wait_ask(t, carry):
        ask_from(peer_slab(t)).wait_recv()
        return carry

    lax.fori_loop(0, count - 1, wait_ask, 0)
    layer = brick_ref.shape[0] * COMP

    def crop(k, target):
        first = pl.multiple_of(k % ZQ * SLAB_Z * layer, 16)
        rows = rows_half[pl.ds(first, (SLAB_Z + 2 * PAD) * layer), :]
        value = crop_rows(asked[k], capacity, rows, select).astype(jnp.bfloat16)
        for part in range(PARTS):
            target[part, k] = value[part * capacity * PART_ROWS:(part + 1) * capacity * PART_ROWS]

    def give(k, part):
        return remote(
            crops.at[part, k], arrived.at[part, me_k],
            crop_send.at[part, k], crop_recv.at[part, me_k], me_s, k,
        )

    def take(k, part):
        return remote(
            crops.at[part, k], arrived.at[part, k],
            crop_send.at[part, k], crop_recv.at[part, k], me_s, k,
        )

    def crop_and_give(t, carry):
        reader = peer_slab(t)
        crop(reader, crops)
        give(reader, 0).start()
        return carry

    lax.fori_loop(0, count - 1, crop_and_give, 0)

    for part in range(1, PARTS):
        def give_part(t, carry):
            give(peer_slab(t), part).start()
            return carry

        lax.fori_loop(0, count - 1, give_part, 0)

    crop(me_k, arrived)
    depth = count * capacity * PART_ROWS

    load_slot.wait()

    def make_hits(row, carry):
        hits[row] = placing_hits(slot_ref, row, depth)
        return carry

    lax.fori_loop(0, subjects, make_hits, 0)

    for t in range(1, subjects):
        u_block_from(peer_subj(t)).wait_recv()

    @pl.when(has_before)
    def _():
        for t in range(subjects):
            u_after(peer_subj(t), peer_subj(t)).wait_recv()

    @pl.when(has_after)
    def _():
        for t in range(subjects):
            u_before(peer_subj(t), peer_subj(t)).wait_recv()

    def rotate(s, carry):
        for z in range(SLAB_Z):
            layers = [
                [u_all[s, a, near].astype(jnp.float32) if 0 <= near < SLAB_Z else None for a in range(3)]
                for near in (z - 1, z, z + 1)
            ]
            beside = [
                [
                    u_rim[s, side, a].astype(jnp.float32)
                    if layers[2 * side][a] is None
                    else layers[2 * side][a][1:BRICK + 1]
                    for a in range(3)
                ]
                for side in range(2)
            ]
            rotation = rotation_at(layers[1], beside[0], beside[1])
            for a in range(3):
                for b in range(3):
                    rotations[s, z, a * 3 + b] = rotation[a][b]
        return carry

    lax.fori_loop(0, subjects, rotate, 0)

    def share(r, part):
        return remote(
            placed.at[r, part], fields.at[me_s, part],
            field_send.at[part, r], field_recv.at[part, me_s], r, me_k,
        )

    def shared_from(s, part):
        return remote(
            placed.at[s, part], fields.at[s, part],
            field_send.at[part, s], field_recv.at[part, s], s, me_k,
        )

    for part in range(PARTS):
        def collect(t, carry):
            take(peer_slab(t), part).wait_recv()
            return carry

        lax.fori_loop(0, count - 1, collect, 0)
        windows = arrived[part].reshape(depth, FLAT)
        for t in range(1, subjects):
            r = peer_subj(t)
            placed[r, part] = place_row(hits[r], windows)
            share(r, part).start()
        fields[me_s, part] = place_row(hits[me_s], windows)

    def add_subject(t, first):
        s = peer_subj(t)

        def step(z, carry):
            rotation = [[rotations[s, z, a * 3 + b] for b in range(3)] for a in range(3)]
            tensor = [
                fields[s, c // PART_COMP, z * PART_COMP + c % PART_COMP].astype(jnp.float32) * (1.0 / subjects)
                for c in range(COMP)
            ]
            rotated = reorient(tensor, rotation)
            for c in range(COMP):
                out_ref[c, z] = rotated[c] if first else out_ref[c, z] + rotated[c]
            return carry

        lax.fori_loop(0, SLAB_Z, step, 0)

    add_subject(0, True)
    for t in range(1, subjects):
        for part in range(PARTS):
            shared_from(peer_subj(t), part).wait_recv()
        add_subject(t, False)

    def finish(t, carry):
        k = peer_slab(t)
        ask(k).wait_send()
        for part in range(PARTS):
            give(k, part).wait_send()
        return carry

    lax.fori_loop(0, count - 1, finish, 0)
    for t in range(1, subjects):
        u_block(peer_subj(t)).wait_send()
        for part in range(PARTS):
            share(peer_subj(t), part).wait_send()

    @pl.when(has_before)
    def _():
        for t in range(subjects):
            u_before(peer_subj(t), me_s).wait_send()

    @pl.when(has_after)
    def _():
        for t in range(subjects):
            u_after(peer_subj(t), me_s).wait_send()


MESH = pl.DeviceIdType.MESH
VMEM_SPEC = pl.BlockSpec(memory_space=pltpu.VMEM)
HBM_SPEC = pl.BlockSpec(memory_space=pltpu.HBM)


def slot_tables(brick_ids, brick_offsets, held, slab_count, capacity):
    wanted = brick_ids[0]
    pieces = wanted.shape[0]
    owner, local = wanted // held, wanted % held
    positions = jnp.arange(pieces, dtype=jnp.int32)
    earlier = (owner[:, None] == owner[None, :]) & (positions[None, :] < positions[:, None])
    slot_of = owner * capacity + jnp.sum(earlier.astype(jnp.int32), axis=1)
    shift = brick_offsets[0, 1] * EDGE + brick_offsets[0, 2]
    code = (local + brick_offsets[0, 0] * held) * COMP * LANES + shift
    hits = slot_of[:, None] == jnp.arange(slab_count * capacity, dtype=jnp.int32)[None, :]
    return slot_of, jnp.sum(jnp.where(hits, code[:, None], 0), axis=0)


def shards(source_bricks, brick_ids, brick_offsets, deformation):
    slab_count, subjects = lax.axis_size("slab"), lax.axis_size("subj")
    pieces = brick_ids.shape[1]
    held = source_bricks.shape[1]
    capacity = max(2, 3 * pieces // (2 * slab_count))
    part_rows = capacity * PART_ROWS
    slot_of, code = slot_tables(brick_ids, brick_offsets, held, slab_count, capacity)
    code = jnp.pad(code.reshape(slab_count, 1, capacity), ((0, 0), (0, 0), (0, LANES - capacity)))
    bf16, f32, dma = jnp.bfloat16, jnp.float32, pltpu.SemaphoreType.DMA
    per_slab, per_subject = dma((slab_count,)), dma((subjects,))
    return pl.pallas_call(
        warp_kernel,
        out_shape=jax.ShapeDtypeStruct((COMP, SLAB_Z, BRICK, LANES), f32),
        in_specs=[HBM_SPEC] * 4,
        out_specs=VMEM_SPEC,
        scratch_shapes=[
            pltpu.VMEM(code.shape, jnp.int32),
            pltpu.SMEM(slot_of.shape, jnp.int32),
            pltpu.VMEM(source_bricks.shape[1:], bf16),
            pltpu.VMEM(deformation.shape[1:], f32),
            pltpu.VMEM((slab_count, 1, LANES), jnp.int32),
            pltpu.VMEM((4, held * BRICK_ROWS, LANES), f32),
            pltpu.VMEM((held * BRICK_ROWS, 4 * LANES), bf16),
            pltpu.VMEM((PARTS, slab_count, part_rows, FLAT), bf16),
            pltpu.VMEM((PARTS, slab_count, part_rows, FLAT), bf16),
            pltpu.VMEM((subjects, LANES // BRICK * PART_ROWS, slab_count * part_rows), bf16),
            pltpu.VMEM((deformation.shape[3] + 16, LANES), f32),
            pltpu.VMEM((subjects, 3, SLAB_Z, BRICK + 2, LANES), bf16),
            pltpu.VMEM((2, subjects, 3, BRICK, LANES), bf16),
            pltpu.VMEM((subjects, 3, SLAB_Z, BRICK + 2, LANES), bf16),
            pltpu.VMEM((subjects, 2, 3, BRICK, LANES), bf16),
            pltpu.VMEM((subjects, SLAB_Z, 9, BRICK, LANES), f32),
            pltpu.VMEM((subjects, PARTS, PART_ROWS, BRICK, LANES), bf16),
            pltpu.VMEM((subjects, PARTS, PART_ROWS, BRICK, LANES), bf16),
            dma((4,)),
            per_slab, per_slab, dma((PARTS, slab_count)), dma((PARTS, slab_count)),
            per_subject, per_subject, per_subject, per_subject,
            per_subject, per_subject, dma((PARTS, subjects)), dma((PARTS, subjects)),
        ],
        compiler_params=pltpu.CompilerParams(
            vmem_limit_bytes=63 << 20, collective_id=0, has_side_effects=True
        ),
    )(code, slot_of, source_bricks, deformation)


def solution(mesh):
    in_specs = (
        P("subj", "slab", None),
        P("subj", "slab"),
        P("subj", None, "slab"),
        P("subj", None, "slab", None, None),
    )
    out_specs = P(None, "slab", "subj", None)
    return jax.shard_map(shards, mesh=mesh, in_specs=in_specs, out_specs=out_specs, check_vma=False)
```

```python
import jax
import jax.numpy as jnp
from jax import lax
from jax.experimental import pallas as pl
from jax.experimental.pallas import tpu as pltpu
from jax.sharding import PartitionSpec as P

COMP = 6
BRICK = 16
PAD = 2
EDGE = BRICK + 2 * PAD
ZQ = 4
NEWTON = 2
SLAB_Z = 4
LANES = 128
ROWS = COMP * SLAB_Z
BRICK_ROWS = COMP * EDGE
PARTS = 1
PART_COMP = COMP // PARTS
PART_ROWS = PART_COMP * SLAB_Z
SPAN = 384
FLAT = BRICK * BRICK


def relayout_bricks(x_ref, rows_ref):
    held = x_ref.shape[0]
    lane = lax.broadcasted_iota(jnp.int32, (held, LANES), 1)
    group_lanes = 8 * EDGE * EDGE

    def step(group, carry):
        for m in range(8):
            cz = group * 8 + m
            row = cz % EDGE * (held * COMP) + cz // EDGE
            shift = 16 * m
            tiles = []
            for j in range(4):
                first = pl.multiple_of(group * group_lanes + (3 * m + j) * LANES, LANES)
                tile = x_ref[:, pl.ds(first, LANES)].astype(jnp.float32)
                tiles.append(pltpu.roll(tile, LANES - shift, 1) if shift else tile)
            for j in range(4):
                value = tiles[j]
                if shift and j < 3:
                    value = jnp.where(lane < LANES - shift, tiles[j], tiles[j + 1])
                rows_ref[j, pl.ds(row, held, stride=COMP), :] = value
        return carry

    lax.fori_loop(0, BRICK_ROWS // 8, step, 0)


def selection():
    source = lax.broadcasted_iota(jnp.int32, (SPAN, FLAT), 0)
    target = lax.broadcasted_iota(jnp.int32, (SPAN, FLAT), 1)
    return (source == target // BRICK * EDGE + target % BRICK).astype(jnp.float32).astype(jnp.bfloat16)


def crop_rows(codes, capacity, rows, select):
    depth = rows.shape[0]
    layer = depth // (SLAB_Z + 2 * PAD)
    row = lax.broadcasted_iota(jnp.int32, (PART_ROWS, depth), 0)
    offset = lax.broadcasted_iota(jnp.int32, (PART_ROWS, depth), 1) - (row // PART_COMP * layer + row % PART_COMP)
    hits, shifts = [], []
    for slot in range(capacity):
        code = codes[:, slot:slot + 1]
        start = lax.shift_right_logical(code, jnp.full(code.shape, 7, jnp.int32))
        hits.append(offset - jnp.broadcast_to(start, (PART_ROWS, depth)))
        shifts.append(jnp.broadcast_to(code & (LANES - 1), (PART_ROWS, LANES)))
    hit = jnp.concatenate(
        [(hits[slot] == PART_COMP * part).astype(jnp.float32) for part in range(PARTS) for slot in range(capacity)],
        axis=0,
    ).astype(jnp.bfloat16)
    shift = jnp.concatenate(shifts * PARTS, axis=0)
    found = jnp.dot(hit, rows, preferred_element_type=jnp.float32)
    tiles = [found[:, j * LANES:(j + 1) * LANES] for j in range(4)]
    for bit in (1, 2, 4, 8, 16, 32, 64):
        taken = (shift & bit) != 0
        tiles = [jnp.where(taken, pltpu.roll(tile, LANES - bit, 1), tile) for tile in tiles]
    inside = lax.broadcasted_iota(jnp.int32, shift.shape, 1) + shift < LANES
    shifted = [jnp.where(inside, tiles[j], tiles[j + 1]).astype(jnp.bfloat16) for j in range(3)]
    return jnp.dot(jnp.concatenate(shifted, axis=1), select, preferred_element_type=jnp.float32)


def swap_groups(value):
    sub = lax.broadcasted_iota(jnp.int32, value.shape, 1)
    group = lax.broadcasted_iota(jnp.int32, value.shape, 2) // BRICK
    for bit in (1, 2, 4):
        from_below = pltpu.roll(pltpu.roll(value, 8 - bit, 1), BRICK * bit, 2)
        if bit == 4:
            from_above = from_below
        else:
            from_above = pltpu.roll(pltpu.roll(value, bit, 1), LANES - BRICK * bit, 2)
        low = (sub & bit) == 0
        same = (sub & bit) == (group & bit)
        value = jnp.where(same, value, jnp.where(low, from_below, from_above))
    return value


def placing_hits(slot_ref, row, depth):
    across = LANES // BRICK
    sub = lax.broadcasted_iota(jnp.int32, (across, depth), 0)
    base = jnp.zeros((across, depth), jnp.int32)
    for j in range(across):
        base = jnp.where(sub == j, slot_ref[row * across + j] * PART_ROWS, base)
    offset = lax.broadcasted_iota(jnp.int32, (across, depth), 1) - base
    return jnp.concatenate(
        [(offset == n).astype(jnp.float32) for n in range(PART_ROWS)], axis=0
    ).astype(jnp.bfloat16)


def place_row(hit, windows):
    pieces = jnp.dot(hit, windows, preferred_element_type=jnp.float32)
    halves = [
        swap_groups(pieces[:, h * LANES:(h + 1) * LANES].reshape(PART_ROWS, 8, LANES))
        for h in range(2)
    ]
    return jnp.concatenate(halves, axis=1).astype(jnp.bfloat16)


def polar_factor(matrix):
    for newton_step in range(NEWTON):
        cofactor = [
            [
                matrix[(a + 1) % 3][(b + 1) % 3] * matrix[(a + 2) % 3][(b + 2) % 3]
                - matrix[(a + 1) % 3][(b + 2) % 3] * matrix[(a + 2) % 3][(b + 1) % 3]
                for b in range(3)
            ]
            for a in range(3)
        ]
        determinant = (
            matrix[0][0] * cofactor[0][0]
            + matrix[0][1] * cofactor[0][1]
            + matrix[0][2] * cofactor[0][2]
        )
        scaling = 0.5 / determinant
        matrix = [
            [0.5 * matrix[a][b] + cofactor[a][b] * scaling for b in range(3)] for a in range(3)
        ]
    return matrix


def reorient(components, rotation):
    tensor_rows = [
        [components[0], components[3], components[4]],
        [components[3], components[1], components[5]],
        [components[4], components[5], components[2]],
    ]
    left_side = [
        [
            rotation[a][0] * tensor_rows[0][b]
            + rotation[a][1] * tensor_rows[1][b]
            + rotation[a][2] * tensor_rows[2][b]
            for b in range(3)
        ]
        for a in range(3)
    ]
    pair_list = ((0, 0), (1, 1), (2, 2), (0, 1), (0, 2), (1, 2))
    return [
        left_side[a][0] * rotation[b][0]
        + left_side[a][1] * rotation[b][1]
        + left_side[a][2] * rotation[b][2]
        for a, b in pair_list
    ]


def rotation_at(centre, before, after):
    lane = lax.broadcasted_iota(jnp.int32, (BRICK, LANES), 1)
    matrix = []
    for a in range(3):
        here = centre[a][1:BRICK + 1]
        along_z = (after[a] - before[a]) * 0.5
        along_y = (centre[a][2:BRICK + 2] - centre[a][0:BRICK]) * 0.5
        later = jnp.where(lane == LANES - 1, 0.0, pltpu.roll(here, LANES - 1, 1))
        earlier = jnp.where(lane == 0, 0.0, pltpu.roll(here, 1, 1))
        gradients = [along_z, along_y, (later - earlier) * 0.5]
        gradients[a] = gradients[a] + 1.0
        matrix.append(gradients)
    return polar_factor(matrix)


def warp_kernel(
    code_ref, slot_ref, brick_hbm, u_hbm, out_ref,
    brick_ref, u_ref, asked, rows_ref, rows_half, crops, arrived, hits,
    u_pad, u_rows, u_edge, u_all, u_rim, rotations, placed, fields, load_sem,
    ask_send, ask_recv, crop_send, crop_recv, u_send, u_recv, up_send, up_recv,
    down_send, down_recv, field_send, field_recv,
):
    count, subjects = arrived.shape[1], fields.shape[0]
    capacity = arrived.shape[2] // PART_ROWS
    load_u = pltpu.make_async_copy(u_hbm.at[0], u_ref, load_sem.at[0])
    load_u.start()
    load_bricks = pltpu.make_async_copy(brick_hbm.at[0], brick_ref, load_sem.at[1])
    load_bricks.start()
    me_s, me_k = lax.axis_index("subj"), lax.axis_index("slab")
    barrier = pltpu.get_barrier_semaphore()
    has_before, has_after = me_k > 0, me_k < count - 1

    def peer_slab(t):
        turn = (t + 1) // 2
        return (me_k + count // 2 + turn * (1 - 2 * ((t + 1) % 2)) + count) % count

    def peer_subj(t):
        return (me_s + t) % subjects

    def greet(s, k):
        pl.semaphore_signal(barrier, inc=1, device_id=(s, k), device_id_type=MESH)

    def greet_slab(t, carry):
        greet(me_s, peer_slab(t))
        return carry

    lax.fori_loop(0, count - 1, greet_slab, 0)
    for t in range(1, subjects):
        greet(peer_subj(t), me_k)

    @pl.when(has_before)
    def _():
        for t in range(1, subjects):
            greet(peer_subj(t), me_k - 1)

    @pl.when(has_after)
    def _():
        for t in range(1, subjects):
            greet(peer_subj(t), me_k + 1)

    def remote(source, target, send, recv, s, k):
        return pltpu.make_async_remote_copy(
            src_ref=source, dst_ref=target, send_sem=send, recv_sem=recv,
            device_id=(s, k), device_id_type=MESH,
        )

    edge = jnp.zeros((8, LANES), jnp.float32)
    height = u_ref.shape[2]
    u_pad[0:8, :] = edge
    u_pad[8 + height:16 + height, :] = edge
    load_u.wait()

    def pad_rows(at, carry):
        a, z = at // SLAB_Z, at % SLAB_Z
        u_pad[8:8 + height, :] = u_ref[a, z]
        for r in range(subjects):
            first = 7 + r * BRICK
            u_rows[r, a, z] = u_pad[first:first + BRICK + 2, :].astype(jnp.bfloat16)
        return carry

    lax.fori_loop(0, 3 * SLAB_Z, pad_rows, 0)
    for side in range(2):
        for a in range(3):
            for r in range(subjects):
                u_edge[side, r, a] = u_ref[
                    a, side * (SLAB_Z - 1), r * BRICK:(r + 1) * BRICK, :
                ].astype(jnp.bfloat16)

    neighbours = (me_k + count - 1) // count + (2 * count - 2 - me_k) // count
    pl.semaphore_wait(barrier, count - 1 + (subjects - 1) * (1 + neighbours))

    def ask(k):
        return remote(code_ref.at[k], asked.at[me_k], ask_send.at[k], ask_recv.at[me_k], me_s, k)

    def ask_from(k):
        return remote(code_ref.at[k], asked.at[k], ask_send.at[k], ask_recv.at[k], me_s, k)

    def start_ask(t, carry):
        ask(peer_slab(t)).start()
        return carry

    lax.fori_loop(0, count - 1, start_ask, 0)
    asked[me_k] = code_ref[me_k]

    def u_block(r):
        return remote(u_rows.at[r], u_all.at[me_s], u_send.at[r], u_recv.at[me_s], r, me_k)

    def u_block_from(s):
        return remote(u_rows.at[s], u_all.at[s], u_send.at[s], u_recv.at[s], s, me_k)

    def u_before(r, s):
        return remote(
            u_edge.at[0, r], u_rim.at[s, 1], up_send.at[r], up_recv.at[s], r, me_k - 1
        )

    def u_after(r, s):
        return remote(
            u_edge.at[1, r], u_rim.at[s, 0], down_send.at[r], down_recv.at[s], r, me_k + 1
        )

    for t in range(1, subjects):
        u_block(peer_subj(t)).start()

    @pl.when(has_before)
    def _():
        for t in range(subjects):
            u_before(peer_subj(t), me_s).start()

    @pl.when(has_after)
    def _():
        for t in range(subjects):
            u_after(peer_subj(t), me_s).start()

    def keep_u(at, carry):
        a, z = at // SLAB_Z, at % SLAB_Z
        u_all[me_s, a, z] = u_rows[me_s, a, z]
        return carry

    lax.fori_loop(0, 3 * SLAB_Z, keep_u, 0)
    rim = jnp.zeros((BRICK, LANES), jnp.bfloat16)

    @pl.when(me_k == 0)
    def _():
        for s in range(subjects):
            for a in range(3):
                u_rim[s, 0, a] = rim

    @pl.when(me_k == count - 1)
    def _():
        for s in range(subjects):
            for a in range(3):
                u_rim[s, 1, a] = rim

    load_bricks.wait()
    relayout_bricks(brick_ref, rows_ref)
    for j in range(4):
        rows_half[:, j * LANES:(j + 1) * LANES] = rows_ref[j].astype(jnp.bfloat16)
    select = selection()

    def wait_ask(t, carry):
        ask_from(peer_slab(t)).wait_recv()
        return carry

    lax.fori_loop(0, count - 1, wait_ask, 0)
    layer = brick_ref.shape[0] * COMP

    def crop(k, target):
        first = pl.multiple_of(k % ZQ * SLAB_Z * layer, 16)
        rows = rows_half[pl.ds(first, (SLAB_Z + 2 * PAD) * layer), :]
        value = crop_rows(asked[k], capacity, rows, select).astype(jnp.bfloat16)
        for part in range(PARTS):
            target[part, k] = value[part * capacity * PART_ROWS:(part + 1) * capacity * PART_ROWS]

    def give(k, part):
        return remote(
            crops.at[part, k], arrived.at[part, me_k],
            crop_send.at[part, k], crop_recv.at[part, me_k], me_s, k,
        )

    def take(k, part):
        return remote(
            crops.at[part, k], arrived.at[part, k],
            crop_send.at[part, k], crop_recv.at[part, k], me_s, k,
        )

    def crop_and_give(t, carry):
        reader = peer_slab(t)
        crop(reader, crops)
        give(reader, 0).start()
        return carry

    lax.fori_loop(0, count - 1, crop_and_give, 0)

    for part in range(1, PARTS):
        def give_part(t, carry):
            give(peer_slab(t), part).start()
            return carry

        lax.fori_loop(0, count - 1, give_part, 0)

    crop(me_k, arrived)
    depth = count * capacity * PART_ROWS

    def make_hits(row, carry):
        hits[row] = placing_hits(slot_ref, row, depth)
        return carry

    lax.fori_loop(0, subjects, make_hits, 0)

    for t in range(1, subjects):
        u_block_from(peer_subj(t)).wait_recv()

    @pl.when(has_before)
    def _():
        for t in range(subjects):
            u_after(peer_subj(t), peer_subj(t)).wait_recv()

    @pl.when(has_after)
    def _():
        for t in range(subjects):
            u_before(peer_subj(t), peer_subj(t)).wait_recv()

    def rotate(s, carry):
        for z in range(SLAB_Z):
            layers = [
                [u_all[s, a, near].astype(jnp.float32) if 0 <= near < SLAB_Z else None for a in range(3)]
                for near in (z - 1, z, z + 1)
            ]
            beside = [
                [
                    u_rim[s, side, a].astype(jnp.float32)
                    if layers[2 * side][a] is None
                    else layers[2 * side][a][1:BRICK + 1]
                    for a in range(3)
                ]
                for side in range(2)
            ]
            rotation = rotation_at(layers[1], beside[0], beside[1])
            for a in range(3):
                for b in range(3):
                    rotations[s, z, a * 3 + b] = rotation[a][b]
        return carry

    lax.fori_loop(0, subjects, rotate, 0)

    def share(r, part):
        return remote(
            placed.at[r, part], fields.at[me_s, part],
            field_send.at[part, r], field_recv.at[part, me_s], r, me_k,
        )

    def shared_from(s, part):
        return remote(
            placed.at[s, part], fields.at[s, part],
            field_send.at[part, s], field_recv.at[part, s], s, me_k,
        )

    for part in range(PARTS):
        def collect(t, carry):
            take(peer_slab(t), part).wait_recv()
            return carry

        lax.fori_loop(0, count - 1, collect, 0)
        windows = arrived[part].reshape(depth, FLAT)
        for t in range(1, subjects):
            r = peer_subj(t)
            placed[r, part] = place_row(hits[r], windows)
            share(r, part).start()
        fields[me_s, part] = place_row(hits[me_s], windows)

    def add_subject(t, first):
        s = peer_subj(t)

        def step(z, carry):
            rotation = [[rotations[s, z, a * 3 + b] for b in range(3)] for a in range(3)]
            tensor = [
                fields[s, c // PART_COMP, z * PART_COMP + c % PART_COMP].astype(jnp.float32) * (1.0 / subjects)
                for c in range(COMP)
            ]
            rotated = reorient(tensor, rotation)
            for c in range(COMP):
                out_ref[c, z] = rotated[c] if first else out_ref[c, z] + rotated[c]
            return carry

        lax.fori_loop(0, SLAB_Z, step, 0)

    add_subject(0, True)
    for t in range(1, subjects):
        for part in range(PARTS):
            shared_from(peer_subj(t), part).wait_recv()
        add_subject(t, False)

    def finish(t, carry):
        k = peer_slab(t)
        ask(k).wait_send()
        for part in range(PARTS):
            give(k, part).wait_send()
        return carry

    lax.fori_loop(0, count - 1, finish, 0)
    for t in range(1, subjects):
        u_block(peer_subj(t)).wait_send()
        for part in range(PARTS):
            share(peer_subj(t), part).wait_send()

    @pl.when(has_before)
    def _():
        for t in range(subjects):
            u_before(peer_subj(t), me_s).wait_send()

    @pl.when(has_after)
    def _():
        for t in range(subjects):
            u_after(peer_subj(t), me_s).wait_send()


MESH = pl.DeviceIdType.MESH
VMEM_SPEC = pl.BlockSpec(memory_space=pltpu.VMEM)
HBM_SPEC = pl.BlockSpec(memory_space=pltpu.HBM)
SMEM_SPEC = pl.BlockSpec(memory_space=pltpu.SMEM)


def slot_tables(brick_ids, brick_offsets, held, slab_count, capacity):
    wanted = brick_ids[0]
    pieces = wanted.shape[0]
    owner, local = wanted // held, wanted % held
    positions = jnp.arange(pieces, dtype=jnp.int32)
    earlier = (owner[:, None] == owner[None, :]) & (positions[None, :] < positions[:, None])
    slot_of = owner * capacity + jnp.sum(earlier.astype(jnp.int32), axis=1)
    shift = brick_offsets[0, 1] * EDGE + brick_offsets[0, 2]
    code = (local + brick_offsets[0, 0] * held) * COMP * LANES + shift
    hits = slot_of[:, None] == jnp.arange(slab_count * capacity, dtype=jnp.int32)[None, :]
    return slot_of, jnp.sum(jnp.where(hits, code[:, None], 0), axis=0)


def shards(source_bricks, brick_ids, brick_offsets, deformation):
    slab_count, subjects = lax.axis_size("slab"), lax.axis_size("subj")
    pieces = brick_ids.shape[1]
    held = source_bricks.shape[1]
    capacity = max(2, 3 * pieces // (2 * slab_count))
    part_rows = capacity * PART_ROWS
    slot_of, code = slot_tables(brick_ids, brick_offsets, held, slab_count, capacity)
    code = jnp.pad(code.reshape(slab_count, 1, capacity), ((0, 0), (0, 0), (0, LANES - capacity)))
    bf16, f32, dma = jnp.bfloat16, jnp.float32, pltpu.SemaphoreType.DMA
    per_slab, per_subject = dma((slab_count,)), dma((subjects,))
    return pl.pallas_call(
        warp_kernel,
        out_shape=jax.ShapeDtypeStruct((COMP, SLAB_Z, BRICK, LANES), f32),
        in_specs=[VMEM_SPEC, SMEM_SPEC, HBM_SPEC, HBM_SPEC],
        out_specs=VMEM_SPEC,
        scratch_shapes=[
            pltpu.VMEM(source_bricks.shape[1:], bf16),
            pltpu.VMEM(deformation.shape[1:], f32),
            pltpu.VMEM((slab_count, 1, LANES), jnp.int32),
            pltpu.VMEM((4, held * BRICK_ROWS, LANES), f32),
            pltpu.VMEM((held * BRICK_ROWS, 4 * LANES), bf16),
            pltpu.VMEM((PARTS, slab_count, part_rows, FLAT), bf16),
            pltpu.VMEM((PARTS, slab_count, part_rows, FLAT), bf16),
            pltpu.VMEM((subjects, LANES // BRICK * PART_ROWS, slab_count * part_rows), bf16),
            pltpu.VMEM((deformation.shape[3] + 16, LANES), f32),
            pltpu.VMEM((subjects, 3, SLAB_Z, BRICK + 2, LANES), bf16),
            pltpu.VMEM((2, subjects, 3, BRICK, LANES), bf16),
            pltpu.VMEM((subjects, 3, SLAB_Z, BRICK + 2, LANES), bf16),
            pltpu.VMEM((subjects, 2, 3, BRICK, LANES), bf16),
            pltpu.VMEM((subjects, SLAB_Z, 9, BRICK, LANES), f32),
            pltpu.VMEM((subjects, PARTS, PART_ROWS, BRICK, LANES), bf16),
            pltpu.VMEM((subjects, PARTS, PART_ROWS, BRICK, LANES), bf16),
            dma((2,)),
            per_slab, per_slab, dma((PARTS, slab_count)), dma((PARTS, slab_count)),
            per_subject, per_subject, per_subject, per_subject,
            per_subject, per_subject, dma((PARTS, subjects)), dma((PARTS, subjects)),
        ],
        compiler_params=pltpu.CompilerParams(
            vmem_limit_bytes=48 << 20, collective_id=0, has_side_effects=True
        ),
    )(code, slot_of, source_bricks, deformation)


def solution(mesh):
    in_specs = (
        P("subj", "slab", None),
        P("subj", "slab"),
        P("subj", None, "slab"),
        P("subj", None, "slab", None, None),
    )
    out_specs = P(None, "slab", "subj", None)
    return jax.shard_map(shards, mesh=mesh, in_specs=in_specs, out_specs=out_specs, check_vma=False)
```
